256 devices in a mesh: ctx: 32 (over y_lo, z, core), seq: 2 (over y_hi), ch: 4 (over x).
Axes of the slice: x: 4, y: 4 (y_hi: 2, y_lo: 2; y = y_hi * 2 + y_lo), z: 8, core: 2. Of those that a mesh axis runs over, the one named last changes fastest.
Arguments:
- grad_out: float32 [2, 512, 16384], P('seq', 'ch', 'ctx'), may hold values from -6 to 6
- query: float32 [2, 512, 16384], P('seq', 'ch', 'ctx'), may hold values from -6 to 6
- keys: float32 [2, 512, 16384], P('seq', 'ch', 'ctx'), may hold values from -6 to 6
- values: float32 [2, 512, 16384], P('seq', 'ch', 'ctx'), may hold values from -6 to 6
- long_filter: float32 [512, 16384], P(('ch', 'ctx')), may hold values from -6 to 6
- short_filter: float32 [512, 3], P('ch'), may hold values from -3.5 to 3.5
Outputs:
- grad_query: float32 [2, 512, 16384], P('seq', 'ch', 'ctx')
- grad_keys: float32 [2, 512, 16384], P('seq', 'ch', 'ctx')
- grad_values: float32 [2, 512, 16384], P('seq', 'ch', 'ctx')
- grad_long: float32 [512, 16384], P(('ch', 'ctx'))
The draws below stay inside these ranges and needn't reach their ends.
All inputs are finite; a program needn't handle non-finite values.
Results may differ from the reference program's by a relative error of at most 0.0001.
Values sent between devices are 32-bit elements; how exact they have to be, the bound alone decides.
No kernel may reach another device: no remote copies, remote signals or barrier semaphores. Data moves between devices by JAX's collectives and lax.ppermute only.
A program may use at most 64 MiB of HBM per device.

```python
import jax
import jax.numpy as jnp
from jax import lax

TAPS = 3
CHANNELS = 512
SEQ_LEN = 16384
SEQS = 2


def levels(key, extent, cuts, low, largest):
    factor_of, own = 1.0, jax.random.fold_in(key, 6)
    for position, blocks in cuts:
        heights = jnp.exp(jax.random.uniform(jax.random.fold_in(own, position), (blocks,), jnp.float32, low / len(cuts), largest / len(cuts)))
        factor_of = factor_of * jnp.repeat(heights, extent[position] // blocks).reshape([-1 if axis == position else 1 for axis in range(len(extent))])
    return factor_of


def centred(key, shape, deviation, limit, cuts=(), held_as=jnp.bfloat16):
    loudness = levels(key, shape, cuts, -0.22, 0.18) if cuts else 1.0
    result = jax.random.normal(key, shape, jnp.float32) * deviation * loudness
    return jnp.minimum(jnp.maximum(result, -limit), limit).astype(held_as)


def setup_inputs(seed: int = 0) -> dict:
    arg_keys = jax.random.split(jax.random.key(seed), 7)
    return {
        "grad_out": centred(arg_keys[0], (SEQS, CHANNELS, SEQ_LEN), 1.0, 6.0, ((0, 2), (1, 4), (2, 32)), jnp.float32),
        "query": centred(arg_keys[1], (SEQS, CHANNELS, SEQ_LEN), 1.0, 6.0, ((0, 2), (1, 4), (2, 32)), jnp.float32),
        "keys": centred(arg_keys[2], (SEQS, CHANNELS, SEQ_LEN), 1.0, 6.0, ((0, 2), (1, 4), (2, 32)), jnp.float32),
        "values": centred(arg_keys[3], (SEQS, CHANNELS, SEQ_LEN), 1.0, 6.0, ((0, 2), (1, 4), (2, 32)), jnp.float32),
        "long_filter": centred(arg_keys[4], (CHANNELS, SEQ_LEN), 1.0, 6.0, ((0, 128),), jnp.float32),
        "short_filter": centred(arg_keys[5], (CHANNELS, TAPS), TAPS ** -0.5, 3.5, ((0, 4),), jnp.float32),
    }


def depthwise(signal, kernel):
    return lax.conv_general_dilated(signal, kernel[:, None, :], (1,), "VALID", dimension_numbers=("NCH", "OIH", "NCH"), feature_group_count=kernel.shape[0], precision=lax.Precision.HIGHEST)


def reference(grad_out, query, keys, values, long_filter, short_filter):
    padded_len = 2 * SEQ_LEN
    scale_factor = SEQ_LEN ** -0.5
    key_window = jnp.pad(keys, ((0, 0), (0, 0), (TAPS - 1, 0)))
    short_keys = depthwise(key_window, jnp.flip(short_filter, 1))
    gated = short_keys * values
    grad_conv = grad_out * query
    spec_gated = jnp.fft.rfft(gated, padded_len, axis=2)
    spec_filter = jnp.fft.rfft(long_filter, padded_len, axis=1)[None]
    spec_grad = jnp.fft.rfft(grad_conv, padded_len, axis=2)
    conv_out = jnp.fft.irfft(spec_gated * spec_filter, padded_len, axis=2)[:, :, :SEQ_LEN] * scale_factor
    grad_gated = jnp.fft.irfft(spec_grad * jnp.conj(spec_filter), padded_len, axis=2)[:, :, :SEQ_LEN] * scale_factor
    cross_spec = jnp.sum(spec_grad * jnp.conj(spec_gated), axis=0)
    grad_long = jnp.fft.irfft(cross_spec, padded_len, axis=1)[:, :SEQ_LEN] * scale_factor
    grad_query = grad_out * conv_out
    grad_short = grad_gated * values
    grad_values = grad_gated * short_keys
    grad_window = jnp.pad(grad_short, ((0, 0), (0, 0), (0, TAPS - 1)))
    grad_keys = depthwise(grad_window, short_filter)
    return grad_query, grad_keys, grad_values, grad_long
```

```python
import functools
import math

import jax
import jax.numpy as jnp
import numpy as np
from jax import lax
from jax.experimental import pallas as pl
from jax.experimental.pallas import tpu as pltpu
from jax.sharding import PartitionSpec as P

LANES = 128
F32 = jnp.float32
BF16 = jnp.bfloat16


def halves(table):
    high = table.astype(np.float32).astype(jnp.bfloat16)
    low = (table - high.astype(np.float64)).astype(np.float32).astype(jnp.bfloat16)
    return high, low


def make_tables(rows, cols):
    length = rows * cols
    shifted = np.arange(rows) + 0.25
    turn_one = 2 * np.pi * np.outer(shifted, np.arange(rows)) / rows
    turn_mid = 2 * np.pi * np.outer(shifted, np.arange(cols)) / length
    turn_two = 2 * np.pi * np.outer(np.arange(cols), np.arange(cols)) / cols
    cos, sin = np.cos(turn_two), np.sin(turn_two)
    first = np.concatenate([np.cos(turn_one), -np.sin(turn_one)], 0)
    second = np.block([[cos, -sin], [sin, cos]])
    second_inv = np.block([[cos, sin], [-sin, cos]])
    scale = length**-1.5
    first_inv = np.concatenate([np.cos(turn_one).T, -np.sin(turn_one).T], 1) * scale
    left = lambda m: np.concatenate([halves(m)[0], halves(m)[0], halves(m)[1]], 1)
    right = lambda m: np.concatenate([halves(m)[0], halves(m)[0], halves(m)[1]], 0)
    mid = np.concatenate([np.cos(turn_mid), -np.sin(turn_mid)], 1).astype(np.float32)
    return left(first), right(second), right(second_inv), left(first_inv), mid


def cut(x):
    high = x.astype(BF16)
    return high, (x - high.astype(F32)).astype(BF16)


def dot(a, b):
    return jnp.dot(a, b, preferred_element_type=F32)


def lane_ids(shape):
    return lax.broadcasted_iota(jnp.int32, shape, len(shape) - 1)


def row_ids(shape):
    return lax.broadcasted_iota(jnp.int32, shape, 0)


def put_cut(lhs, row, re, im):
    n = re.shape[0]
    re_hi, re_lo = cut(re)
    im_hi, im_lo = cut(im)
    for place, piece in enumerate((re_hi, im_hi, re_lo, im_lo, re_hi, im_hi)):
        lhs[pl.ds(row, n), pl.ds(place * LANES, LANES)] = piece


def forward(signals, first, second, mid, lhs, row):
    rows = signals[0].shape[0]
    turn_re = mid[:, :LANES]
    turn_im = mid[:, LANES:]
    for pair in range(0, len(signals), 2):
        hi, lo = cut(jnp.concatenate(signals[pair : pair + 2], 1))
        part = dot(first[...], jnp.concatenate([hi, lo, hi], 0))
        for which in range(2):
            re = part[:rows, which * LANES : (which + 1) * LANES]
            im = part[rows:, which * LANES : (which + 1) * LANES]
            put_cut(
                lhs,
                row + (pair + which) * rows,
                re * turn_re - im * turn_im,
                re * turn_im + im * turn_re,
            )
    return dot(lhs[pl.ds(row, len(signals) * rows), :], second[...])


def backward(count, rows, second_inv, first_inv, mid, lhs, row):
    turn_re = mid[:, :LANES]
    turn_im = mid[:, LANES:]
    back = dot(lhs[pl.ds(row, count * rows), :], second_inv[...])
    pairs = []
    for pair in range(0, count, 2):
        columns = []
        for which in range(2):
            here = back[(pair + which) * rows : (pair + which + 1) * rows]
            re, im = here[:, :LANES], here[:, LANES:]
            columns.append(
                jnp.concatenate([re * turn_re + im * turn_im, im * turn_re - re * turn_im], 0)
            )
        hi, lo = cut(jnp.concatenate(columns, 1))
        out = dot(first_inv[...], jnp.concatenate([hi, lo, hi], 0))
        pairs += [out[:, :LANES], out[:, LANES:]]
    return pairs


def short_taps(keys, taps):
    lane = lane_ids(keys.shape)
    once = jnp.where(lane < 1, 0.0, pltpu.roll(keys, 1, 1))
    twice = jnp.where(lane < 2, 0.0, pltpu.roll(keys, 2, 1))
    return taps[:, 0:1] * keys + taps[:, 1:2] * once + taps[:, 2:3] * twice


def pack_body(own, blocks, grad_out, query, keys, values, taps, out, scratch):
    width = 2 * own + 1
    chunk = width * blocks
    key, value, tap = keys[0], values[0], taps[...]
    chans, span = key.shape
    peers = chans // own
    gated = short_taps(key, tap) * value
    grad = grad_out[0] * query[0]
    lane = lane_ids((chans, LANES))
    tail = key[:, span - LANES :]
    after = tap[:, 2:3] * pltpu.roll(tail, 2, 1) + jnp.where(
        lane < 1, tap[:, 1:2] * pltpu.roll(tail, 1, 1), 0.0
    )
    head = jnp.where(lane < 4, pltpu.roll(value[:, :LANES], 2, 1), 0.0)
    out[pl.ds(2 * own, chans, stride=width), :] = jnp.where(lane < 2, after, head)
    for t, whole in enumerate((gated, grad)):
        for j in range(blocks):
            scratch[t, j] = whole[:, j * LANES : (j + 1) * LANES]
    for t in range(2):
        for j in range(blocks):
            for c in range(own):
                out[pl.ds(width * j + own * t + c, peers, stride=chunk), :] = scratch[
                    t, j, pl.ds(c, peers, stride=own), :
                ]


def filter_body(long_filter, first, second, mid, spec, scratch, lhs):
    own, length = long_filter.shape
    rows = length // LANES
    for n in range(rows):
        scratch[pl.ds(own * n, own), :] = long_filter[:, pl.ds(n * LANES, LANES)]
    signals = [scratch[pl.ds(c, rows, stride=own), :] for c in range(own)]
    spec[...] = forward(signals, first, second, mid, lhs, 0)


def main_body(
    own, blocks, recv, filt, first, second, second_inv, first_inv, mid, out, cross, edge, tile, lhs
):
    width = 2 * own + 1
    rows = recv.shape[0] // width
    peers = rows // blocks
    ext = recv[pl.ds(2 * own, rows, stride=width), :]
    lane, line = lane_ids(ext.shape), row_ids(ext.shape)
    heads = pltpu.roll(ext, LANES - 2, 1)
    before = jnp.where(line < own, 0.0, pltpu.roll(ext, own, 0))
    edge[...] = jnp.where(lane < 2, heads * before, 0.0)
    for c in range(own):
        tile[c] = recv[pl.ds(c, rows, stride=width), :]
        tile[c, pl.ds(0, peers, stride=blocks), :] += edge[pl.ds(c, peers, stride=own), :]
    gate = forward([tile[c] for c in range(own)], first, second, mid, lhs, 0)
    grads = [recv[pl.ds(own + c, rows, stride=width), :] for c in range(own)]
    grad = forward(grads, first, second, mid, lhs, own * rows)
    for c in range(own):
        here = slice(c * rows, (c + 1) * rows)
        g_re, g_im = gate[here, :LANES], gate[here, LANES:]
        d_re, d_im = grad[here, :LANES], grad[here, LANES:]
        f_re, f_im = filt[here, :LANES], filt[here, LANES:]
        put_cut(lhs, c * rows, g_re * f_re - g_im * f_im, g_re * f_im + g_im * f_re)
        put_cut(lhs, (own + c) * rows, d_re * f_re + d_im * f_im, d_im * f_re - d_re * f_im)
        cross[here, :LANES] = d_re * g_re + d_im * g_im
        cross[here, LANES:] = d_im * g_re - d_re * g_im
    signals = backward(2 * own, rows, second_inv, first_inv, mid, lhs, 0)
    for q, signal in enumerate(signals):
        out[pl.ds(q, rows, stride=width), :] = signal
    for c in range(own):
        tile[c] = signals[own + c]
        edge[pl.ds(c, peers, stride=own), :] = tile[c, pl.ds(0, peers, stride=blocks), :]
    behind = jnp.where(line < rows - own, pltpu.roll(edge[...] * heads, rows - own, 0), 0.0)
    shifted = jnp.where(lane < 4, pltpu.roll(before, 2, 1), 0.0)
    out[pl.ds(2 * own, rows, stride=width), :] = jnp.where(lane < 2, behind, shifted)


def cross_body(cross, second_inv, first_inv, mid, part, scratch, lhs):
    own, length = part.shape
    rows = length // LANES
    for c in range(own):
        here = slice(c * rows, (c + 1) * rows)
        put_cut(lhs, c * rows, cross[here, :LANES], cross[here, LANES:])
    for c, signal in enumerate(backward(own, rows, second_inv, first_inv, mid, lhs, 0)):
        scratch[pl.ds(c, rows, stride=own), :] = signal
    for n in range(rows):
        part[:, pl.ds(n * LANES, LANES)] = scratch[pl.ds(own * n, own), :]


def finish_body(
    own, blocks, recv, grad_out, keys, values, taps, grad_query, grad_keys, grad_values, scratch
):
    width = 2 * own + 1
    chunk = width * blocks
    key, value, tap = keys[0], values[0], taps[...]
    chans, span = key.shape
    peers = chans // own
    for t in range(2):
        for j in range(blocks):
            for c in range(own):
                scratch[t, j, pl.ds(c, peers, stride=own), :] = recv[
                    pl.ds(width * j + own * t + c, peers, stride=chunk), :
                ]
    conv = jnp.concatenate([scratch[0, j] for j in range(blocks)], 1)
    grad = jnp.concatenate([scratch[1, j] for j in range(blocks)], 1)
    ext = recv[pl.ds(2 * own, chans, stride=width), :]
    lane = lane_ids((chans, LANES))
    turned = pltpu.roll(ext, LANES - 2, 1)
    grad_query[0] = grad_out[0] * conv
    short = short_taps(key, tap)
    fixed = short[:, :LANES] + jnp.where(lane < 2, turned, 0.0)
    short = jnp.concatenate([fixed, short[:, LANES:]], 1)
    grad_values[0] = grad * short
    part = grad * value
    once = pltpu.roll(part, span - 1, 1)
    twice = pltpu.roll(part, span - 2, 1)
    last = span - LANES
    once_end = jnp.where(lane < LANES - 1, once[:, last:], pltpu.roll(ext, LANES - 1, 1))
    twice_end = jnp.where(lane < LANES - 2, twice[:, last:], turned)
    once = jnp.concatenate([once[:, :last], once_end], 1)
    twice = jnp.concatenate([twice[:, :last], twice_end], 1)
    grad_keys[0] = tap[:, 0:1] * part + tap[:, 1:2] * once + tap[:, 2:3] * twice


def call(body, name, outs, scratch, args, flops):
    moved = sum(a.size * a.dtype.itemsize for a in args) + sum(
        math.prod(o.shape) * o.dtype.itemsize for o in outs
    )
    return pl.pallas_call(
        body,
        out_shape=outs,
        scratch_shapes=scratch,
        name=name,
        cost_estimate=pl.CostEstimate(flops=flops, bytes_accessed=moved, transcendentals=0),
        compiler_params=pltpu.CompilerParams(vmem_limit_bytes=32 * 2**20),
    )(*args)


def shape(*dims):
    return jax.ShapeDtypeStruct(dims, F32)


def exchange(x, parts):
    rows = x.shape[0] // parts
    assert rows % 4 == 0
    moved = x.reshape(parts, rows // 4, 4, LANES)
    moved = lax.all_to_all(moved, "ctx", split_axis=0, concat_axis=0, tiled=True)
    return moved.reshape(x.shape)


def shards(grad_out, query, keys, values, long_filter, short_filter):
    _, chans, span = keys.shape
    own, length = long_filter.shape
    parts = length // span
    blocks = span // LANES
    rows = length // LANES
    assert chans == own * parts and rows == LANES and blocks == own
    packed_rows = parts * blocks * (2 * own + 1)
    tables = make_tables(rows, LANES)
    first, second, second_inv, first_inv, mid = (jnp.asarray(t) for t in tables)
    wide = 6 * LANES
    work = 6 * own * rows * wide * 2 * LANES
    tiles = pltpu.VMEM((2, blocks, chans, LANES), F32)
    packed = call(
        functools.partial(pack_body, own, blocks),
        "pack",
        (shape(packed_rows, LANES),),
        [tiles],
        (grad_out, query, keys, values, short_filter),
        10 * chans * span,
    )[0]
    received = exchange(packed, parts)
    spec = call(
        filter_body,
        "filter_spectrum",
        (shape(own * rows, 2 * LANES),),
        [pltpu.VMEM((own * rows, LANES), F32), pltpu.VMEM((own * rows, wide), BF16)],
        (long_filter, first, second, mid),
        work,
    )[0]
    sent, cross = call(
        functools.partial(main_body, own, blocks),
        "main",
        (shape(packed_rows, LANES), shape(own * rows, 2 * LANES)),
        [
            pltpu.VMEM((rows, LANES), F32),
            pltpu.VMEM((own, rows, LANES), F32),
            pltpu.VMEM((2 * own * rows, wide), BF16),
        ],
        (received, spec, first, second, second_inv, first_inv, mid),
        4 * work,
    )
    returned = exchange(sent, parts)
    part = call(
        cross_body,
        "cross",
        (shape(own, length),),
        [pltpu.VMEM((own * rows, LANES), F32), pltpu.VMEM((own * rows, wide), BF16)],
        (cross, second_inv, first_inv, mid),
        work,
    )[0]
    grad_long = part + lax.ppermute(part, "seq", [(0, 1), (1, 0)])
    grad_query, grad_keys, grad_values = call(
        functools.partial(finish_body, own, blocks),
        "finish",
        (shape(*keys.shape),) * 3,
        [tiles],
        (returned, grad_out, keys, values, short_filter),
        10 * chans * span,
    )
    return grad_query, grad_keys, grad_values, grad_long


def solution(mesh):
    block = P("seq", "ch", "ctx")
    rows = P(("ch", "ctx"), None)
    return jax.shard_map(
        shards,
        mesh=mesh,
        in_specs=(block, block, block, block, rows, P("ch", None)),
        out_specs=(block, block, block, rows),
        check_vma=False,
    )
```

```python
import functools
import math

import jax
import jax.numpy as jnp
import numpy as np
from jax import lax
from jax.experimental import pallas as pl
from jax.experimental.pallas import tpu as pltpu
from jax.sharding import PartitionSpec as P

LANES = 128
F32 = jnp.float32
BF16 = jnp.bfloat16


def halves(table):
    high = table.astype(np.float32).astype(jnp.bfloat16)
    low = (table - high.astype(np.float64)).astype(np.float32).astype(jnp.bfloat16)
    return high, low


def row_order(rows, blocks):
    return np.arange(rows).reshape(-1, blocks).T.reshape(-1)


def make_tables(rows, cols, order):
    length = rows * cols
    shifted = np.arange(rows) + 0.25
    turn_one = 2 * np.pi * np.outer(shifted, order) / rows
    turn_mid = 2 * np.pi * np.outer(shifted, np.arange(cols)) / length
    turn_two = 2 * np.pi * np.outer(np.arange(cols), np.arange(cols)) / cols
    cos, sin = np.cos(turn_two), np.sin(turn_two)
    first = np.concatenate([np.cos(turn_one), -np.sin(turn_one)], 0)
    second = np.block([[cos, -sin], [sin, cos]])
    second_inv = np.block([[cos, sin], [-sin, cos]])
    scale = length**-1.5
    first_inv = np.concatenate([np.cos(turn_one).T, -np.sin(turn_one).T], 1) * scale
    left = lambda m: np.concatenate([halves(m)[0], halves(m)[0], halves(m)[1]], 1)
    right = lambda m: np.concatenate([halves(m)[0], halves(m)[0], halves(m)[1]], 0)
    mid = np.concatenate([np.cos(turn_mid), -np.sin(turn_mid)], 1).astype(np.float32)
    return left(first), right(second), right(second_inv), left(first_inv), mid


def cut(x):
    high = x.astype(BF16)
    return high, (x - high.astype(F32)).astype(BF16)


def dot(a, b):
    return jnp.dot(a, b, preferred_element_type=F32)


def lane_ids(shape):
    return lax.broadcasted_iota(jnp.int32, shape, len(shape) - 1)


def row_ids(shape):
    return lax.broadcasted_iota(jnp.int32, shape, 0)


def put_cut(lhs, row, re, im):
    n = re.shape[0]
    re_hi, re_lo = cut(re)
    im_hi, im_lo = cut(im)
    for place, piece in enumerate((re_hi, im_hi, re_lo, im_lo, re_hi, im_hi)):
        lhs[pl.ds(row, n), pl.ds(place * LANES, LANES)] = piece


def forward(signals, first, second, mid, lhs, row):
    rows = signals[0].shape[0]
    turn_re = mid[:, :LANES]
    turn_im = mid[:, LANES:]
    for pair in range(0, len(signals), 2):
        hi, lo = cut(jnp.concatenate(signals[pair : pair + 2], 1))
        part = dot(first[...], jnp.concatenate([hi, lo, hi], 0))
        for which in range(2):
            re = part[:rows, which * LANES : (which + 1) * LANES]
            im = part[rows:, which * LANES : (which + 1) * LANES]
            put_cut(
                lhs,
                row + (pair + which) * rows,
                re * turn_re - im * turn_im,
                re * turn_im + im * turn_re,
            )
    return dot(lhs[pl.ds(row, len(signals) * rows), :], second[...])


def backward(count, rows, second_inv, first_inv, mid, lhs, row):
    turn_re = mid[:, :LANES]
    turn_im = mid[:, LANES:]
    back = dot(lhs[pl.ds(row, count * rows), :], second_inv[...])
    pairs = []
    for pair in range(0, count, 2):
        columns = []
        for which in range(2):
            here = back[(pair + which) * rows : (pair + which + 1) * rows]
            re, im = here[:, :LANES], here[:, LANES:]
            columns.append(
                jnp.concatenate([re * turn_re + im * turn_im, im * turn_re - re * turn_im], 0)
            )
        hi, lo = cut(jnp.concatenate(columns, 1))
        out = dot(first_inv[...], jnp.concatenate([hi, lo, hi], 0))
        pairs += [out[:, :LANES], out[:, LANES:]]
    return pairs


def tap_tiles(taps):
    chans = taps.shape[1]
    return [
        jnp.transpose(jnp.broadcast_to(taps[j : j + 1, :], (LANES, chans)))
        for j in range(taps.shape[0])
    ]


def short_taps(keys, taps):
    lane = lane_ids(keys.shape)
    once = jnp.where(lane < 1, 0.0, pltpu.roll(keys, 1, 1))
    twice = jnp.where(lane < 2, 0.0, pltpu.roll(keys, 2, 1))
    wide = [jnp.concatenate([t] * (keys.shape[1] // LANES), 1) for t in taps]
    return wide[0] * keys + wide[1] * once + wide[2] * twice


def pack_body(
    own, blocks, grad_out, query, keys, values, taps, out, held, scratch, edge, sems
):
    copies = [
        pltpu.make_async_copy(source.at[0], held.at[i], sems.at[i])
        for i, source in enumerate((keys, values, grad_out, query))
    ]
    for copy in copies:
        copy.start()
    chunk = 2 * own * blocks + 1
    tap = tap_tiles(taps)
    chans, span = keys.shape[1:]
    peers = chans // own
    copies[0].wait()
    copies[1].wait()
    key, value = held[0], held[1]
    gated = short_taps(key, tap) * value
    lane = lane_ids((chans, LANES))
    tail = key[:, span - LANES :]
    after = tap[2] * pltpu.roll(tail, 2, 1) + jnp.where(
        lane < 1, tap[1] * pltpu.roll(tail, 1, 1), 0.0
    )
    head = jnp.where(lane < 4, pltpu.roll(value[:, :LANES], 2, 1), 0.0)
    edge[...] = jnp.where(lane < 2, after, head)
    ends = edge[pl.ds(0, peers, stride=own), :]
    for c in range(1, own):
        ends = ends + pltpu.roll(edge[pl.ds(c, peers, stride=own), :], 4 * c, 1)
    out[pl.ds(chunk - 1, peers, stride=chunk), :] = ends
    for t in range(2):
        if t == 1:
            copies[2].wait()
            copies[3].wait()
            gated = held[2] * held[3]
        for j in range(blocks):
            scratch[t, j] = gated[:, j * LANES : (j + 1) * LANES]
            for c in range(own):
                out[pl.ds(2 * own * j + own * t + c, peers, stride=chunk), :] = scratch[
                    t, j, pl.ds(c, peers, stride=own), :
                ]


def filter_body(order, long_filter, first, second, mid, spec, scratch, lhs):
    own, length = long_filter.shape
    rows = length // LANES
    for n, place in enumerate(order):
        scratch[pl.ds(own * n, own), :] = long_filter[:, pl.ds(place * LANES, LANES)]
    signals = [scratch[pl.ds(c, rows, stride=own), :] for c in range(own)]
    spec[...] = forward(signals, first, second, mid, lhs, 0)


def main_body(
    own, blocks, recv, filt, first, second, second_inv, first_inv, mid, out, cross, lhs
):
    chunk = 2 * own * blocks + 1
    peers = recv.shape[0] // chunk
    rows = peers * blocks
    place = lambda t, j, c: pl.ds(2 * own * j + own * t + c, peers, stride=chunk)
    ends = recv[pl.ds(chunk - 1, peers, stride=chunk), :]
    lane, line = lane_ids(ends.shape), row_ids(ends.shape)
    heads, before, gates, grads = [], [], [], []
    for c in range(own):
        heads.append(pltpu.roll(ends, (LANES - 4 * c - 2) % LANES, 1))
        past = pltpu.roll(ends, (LANES - 4 * c) % LANES, 1) if c else ends
        before.append(jnp.where(line < 1, 0.0, pltpu.roll(past, 1, 0)))
        tiles = [recv[place(0, j, c), :] for j in range(blocks)]
        tiles[0] = tiles[0] + jnp.where(lane < 2, heads[c] * before[c], 0.0)
        gates.append(jnp.concatenate(tiles, 0))
        grads.append(jnp.concatenate([recv[place(1, j, c), :] for j in range(blocks)], 0))
    gate = forward(gates, first, second, mid, lhs, 0)
    grad = forward(grads, first, second, mid, lhs, own * rows)
    for c in range(own):
        here = slice(c * rows, (c + 1) * rows)
        g_re, g_im = gate[here, :LANES], gate[here, LANES:]
        d_re, d_im = grad[here, :LANES], grad[here, LANES:]
        f_re, f_im = filt[here, :LANES], filt[here, LANES:]
        put_cut(lhs, c * rows, g_re * f_re - g_im * f_im, g_re * f_im + g_im * f_re)
        put_cut(lhs, (own + c) * rows, d_re * f_re + d_im * f_im, d_im * f_re - d_re * f_im)
        cross[here, :LANES] = d_re * g_re + d_im * g_im
        cross[here, LANES:] = d_im * g_re - d_re * g_im
    signals = backward(2 * own, rows, second_inv, first_inv, mid, lhs, 0)
    for q, signal in enumerate(signals):
        for j in range(blocks):
            out[place(q // own, j, q % own), :] = signal[j * peers : (j + 1) * peers]
    ends = jnp.zeros(ends.shape, F32)
    for c in range(own):
        first_row = signals[own + c][:peers] * heads[c]
        behind = jnp.where(line < peers - 1, pltpu.roll(first_row, peers - 1, 0), 0.0)
        shifted = jnp.where(lane < 4, pltpu.roll(before[c], 2, 1), 0.0)
        mine = jnp.where(lane < 2, behind, shifted)
        ends = ends + (pltpu.roll(mine, 4 * c, 1) if c else mine)
    out[pl.ds(chunk - 1, peers, stride=chunk), :] = ends


def cross_body(order, cross, second_inv, first_inv, mid, part, scratch, lhs):
    own, length = part.shape
    rows = length // LANES
    for c in range(own):
        here = slice(c * rows, (c + 1) * rows)
        put_cut(lhs, c * rows, cross[here, :LANES], cross[here, LANES:])
    for c, signal in enumerate(backward(own, rows, second_inv, first_inv, mid, lhs, 0)):
        scratch[pl.ds(c, rows, stride=own), :] = signal
    for n, place in enumerate(order):
        part[:, pl.ds(place * LANES, LANES)] = scratch[pl.ds(own * n, own), :]


def finish_body(
    own, blocks, recv, grad_out, keys, values, taps, grad_query, grad_keys, grad_values, scratch, edge
):
    chunk = 2 * own * blocks + 1
    key, value, tap = keys[0], values[0], tap_tiles(taps)
    chans, span = key.shape
    peers = chans // own
    for t in range(2):
        for j in range(blocks):
            for c in range(own):
                scratch[t, j, pl.ds(c, peers, stride=own), :] = recv[
                    pl.ds(2 * own * j + own * t + c, peers, stride=chunk), :
                ]
    conv = jnp.concatenate([scratch[0, j] for j in range(blocks)], 1)
    grad = jnp.concatenate([scratch[1, j] for j in range(blocks)], 1)
    ends = recv[pl.ds(chunk - 1, peers, stride=chunk), :]
    for c in range(own):
        edge[pl.ds(c, peers, stride=own), :] = (
            pltpu.roll(ends, (LANES - 4 * c) % LANES, 1) if c else ends
        )
    ext = edge[...]
    lane = lane_ids((chans, LANES))
    turned = pltpu.roll(ext, LANES - 2, 1)
    grad_query[0] = grad_out[0] * conv
    short = short_taps(key, tap)
    fixed = short[:, :LANES] + jnp.where(lane < 2, turned, 0.0)
    short = jnp.concatenate([fixed, short[:, LANES:]], 1)
    grad_values[0] = grad * short
    part = grad * value
    once = pltpu.roll(part, span - 1, 1)
    twice = pltpu.roll(part, span - 2, 1)
    last = span - LANES
    once_end = jnp.where(lane < LANES - 1, once[:, last:], pltpu.roll(ext, LANES - 1, 1))
    twice_end = jnp.where(lane < LANES - 2, twice[:, last:], turned)
    once = jnp.concatenate([once[:, :last], once_end], 1)
    twice = jnp.concatenate([twice[:, :last], twice_end], 1)
    wide = [jnp.concatenate([t] * blocks, 1) for t in tap]
    grad_keys[0] = wide[0] * part + wide[1] * once + wide[2] * twice


def call(body, name, outs, scratch, args, flops, in_specs=None, room=32):
    moved = sum(a.size * a.dtype.itemsize for a in args) + sum(
        math.prod(o.shape) * o.dtype.itemsize for o in outs
    )
    return pl.pallas_call(
        body,
        out_shape=outs,
        scratch_shapes=scratch,
        name=name,
        **({} if in_specs is None else {"in_specs": in_specs}),
        cost_estimate=pl.CostEstimate(flops=flops, bytes_accessed=moved, transcendentals=0),
        compiler_params=pltpu.CompilerParams(vmem_limit_bytes=room * 2**20),
    )(*args)


def shape(*dims):
    return jax.ShapeDtypeStruct(dims, F32)


def exchange(x, parts):
    moved = x.reshape(parts, x.shape[0] // parts, 1, LANES)
    moved = lax.all_to_all(moved, "ctx", split_axis=0, concat_axis=0, tiled=True)
    return moved.reshape(x.shape)


def shards(grad_out, query, keys, values, long_filter, short_filter):
    _, chans, span = keys.shape
    own, length = long_filter.shape
    parts = length // span
    blocks = span // LANES
    rows = length // LANES
    assert chans == own * parts and rows == LANES and blocks == own
    packed_rows = parts * (2 * own * blocks + 1)
    order = row_order(rows, blocks)
    places = tuple(int(n) for n in order)
    tables = make_tables(rows, LANES, order)
    taps = short_filter.T
    first, second, second_inv, first_inv, mid = (jnp.asarray(t) for t in tables)
    wide = 6 * LANES
    work = 6 * own * rows * wide * 2 * LANES
    tiles = pltpu.VMEM((2, blocks, chans, LANES), F32)
    packed = call(
        functools.partial(pack_body, own, blocks),
        "pack",
        (shape(packed_rows, LANES),),
        [
            pltpu.VMEM((4, chans, span), F32),
            tiles,
            pltpu.VMEM((chans, LANES), F32),
            pltpu.SemaphoreType.DMA((4,)),
        ],
        (grad_out, query, keys, values, taps),
        10 * chans * span,
        [pl.BlockSpec(memory_space=pltpu.HBM)] * 4 + [pl.BlockSpec(memory_space=pltpu.VMEM)],
        60,
    )[0]
    received = exchange(packed, parts)
    spec = call(
        functools.partial(filter_body, places),
        "filter_spectrum",
        (shape(own * rows, 2 * LANES),),
        [pltpu.VMEM((own * rows, LANES), F32), pltpu.VMEM((own * rows, wide), BF16)],
        (long_filter, first, second, mid),
        work,
    )[0]
    sent, cross = call(
        functools.partial(main_body, own, blocks),
        "main",
        (shape(packed_rows, LANES), shape(own * rows, 2 * LANES)),
        [pltpu.VMEM((2 * own * rows, wide), BF16)],
        (received, spec, first, second, second_inv, first_inv, mid),
        4 * work,
    )
    returned = exchange(sent, parts)
    part = call(
        functools.partial(cross_body, places),
        "cross",
        (shape(own, length),),
        [pltpu.VMEM((own * rows, LANES), F32), pltpu.VMEM((own * rows, wide), BF16)],
        (cross, second_inv, first_inv, mid),
        work,
    )[0]
    grad_long = part + lax.ppermute(part, "seq", [(0, 1), (1, 0)])
    grad_query, grad_keys, grad_values = call(
        functools.partial(finish_body, own, blocks),
        "finish",
        (shape(*keys.shape),) * 3,
        [tiles, pltpu.VMEM((chans, LANES), F32)],
        (returned, grad_out, keys, values, taps),
        10 * chans * span,
    )
    return grad_query, grad_keys, grad_values, grad_long


def solution(mesh):
    block = P("seq", "ch", "ctx")
    rows = P(("ch", "ctx"), None)
    return jax.shard_map(
        shards,
        mesh=mesh,
        in_specs=(block, block, block, block, rows, P("ch", None)),
        out_specs=(block, block, block, rows),
        check_vma=False,
    )
```

```python
import functools
import math

import jax
import jax.numpy as jnp
import numpy as np
from jax import lax
from jax.experimental import pallas as pl
from jax.experimental.pallas import tpu as pltpu
from jax.sharding import PartitionSpec as P

LANES = 128
F32 = jnp.float32
BF16 = jnp.bfloat16


def halves(table):
    high = table.astype(np.float32).astype(jnp.bfloat16)
    low = (table - high.astype(np.float64)).astype(np.float32).astype(jnp.bfloat16)
    return high, low


CORES = 2


def peer_order(parts):
    planes = parts // CORES // 2
    chips = [y * planes + z for z in reversed(range(planes)) for y in range(2)]
    return [CORES * chip + core for chip in chips for core in range(CORES)]


def row_order(order, blocks):
    return [blocks * s + j for j in range(blocks) for s in order]


def sorted_rows(x, order, own, back=False):
    size = CORES * own
    chips = [s // CORES for s in order[::CORES]]
    assert [CORES * chip + core for chip in chips for core in range(CORES)] == list(order)
    if back:
        chips = [chips.index(k) for k in range(len(chips))]
    return jnp.concatenate([x[size * k : size * (k + 1)] for k in chips], 0)


def make_tables(rows, cols, order):
    length = rows * cols
    shifted = np.arange(rows) + 0.25
    turn_one = 2 * np.pi * np.outer(shifted, np.array(order)) / rows
    turn_mid = 2 * np.pi * np.outer(shifted, np.arange(cols)) / length
    turn_two = 2 * np.pi * np.outer(np.arange(cols), np.arange(cols)) / cols
    cos, sin = np.cos(turn_two), np.sin(turn_two)
    first = np.concatenate([np.cos(turn_one), -np.sin(turn_one)], 0)
    second = np.block([[cos, -sin], [sin, cos]])
    second_inv = np.block([[cos, sin], [-sin, cos]])
    scale = length**-1.5
    first_inv = np.concatenate([np.cos(turn_one).T, -np.sin(turn_one).T], 1) * scale
    both = lambda m: np.concatenate(halves(m), 0)
    right = lambda m: np.concatenate([halves(m)[0], halves(m)[0], halves(m)[1]], 0)
    mid = np.concatenate([np.cos(turn_mid), -np.sin(turn_mid)], 1).astype(np.float32)
    left = lambda m: np.concatenate([halves(m)[0], halves(m)[0], halves(m)[1]], 1)
    return left(first), right(second), right(second_inv), both(first_inv), mid


def cut(x):
    high = x.astype(BF16)
    return high, (x - high.astype(F32)).astype(BF16)


def dot(a, b):
    return jnp.dot(a, b, preferred_element_type=F32)


def lane_ids(shape):
    return lax.broadcasted_iota(jnp.int32, shape, len(shape) - 1)


def row_ids(shape):
    return lax.broadcasted_iota(jnp.int32, shape, 0)


def put_cut(lhs, row, re, im):
    n = re.shape[0]
    re_hi, re_lo = cut(re)
    im_hi, im_lo = cut(im)
    for place, piece in enumerate((re_hi, im_hi, re_lo, im_lo, re_hi, im_hi)):
        lhs[pl.ds(row, n), pl.ds(place * LANES, LANES)] = piece


def left_dot(table, x):
    hi, lo = cut(x)
    rows = table.shape[0] // 2
    twice = dot(table[...], hi)
    return twice[:rows] + (twice[rows:] + dot(table[:rows], lo))


def forward(signals, first, second, mid, lhs, row):
    rows = signals[0].shape[0]
    turn_re = mid[:, :LANES]
    turn_im = mid[:, LANES:]
    for pair in range(0, len(signals), 2):
        hi, lo = cut(jnp.concatenate(signals[pair : pair + 2], 1))
        part = dot(first[...], jnp.concatenate([hi, lo, hi], 0))
        for which in range(2):
            re = part[:rows, which * LANES : (which + 1) * LANES]
            im = part[rows:, which * LANES : (which + 1) * LANES]
            put_cut(
                lhs,
                row + (pair + which) * rows,
                re * turn_re - im * turn_im,
                re * turn_im + im * turn_re,
            )
    return dot(lhs[pl.ds(row, len(signals) * rows), :], second[...])


def backward(count, rows, second_inv, first_inv, mid, lhs, row):
    turn_re = mid[:, :LANES]
    turn_im = mid[:, LANES:]
    back = dot(lhs[pl.ds(row, count * rows), :], second_inv[...])
    signals = []
    for pair in range(0, count, 2):
        columns = []
        for which in range(2):
            here = back[(pair + which) * rows : (pair + which + 1) * rows]
            re, im = here[:, :LANES], here[:, LANES:]
            columns.append(
                jnp.concatenate([re * turn_re + im * turn_im, im * turn_re - re * turn_im], 0)
            )
        out = left_dot(first_inv, jnp.concatenate(columns, 1))
        signals += [out[:, :LANES], out[:, LANES:]]
    return signals


def tap_tiles(taps):
    chans = taps.shape[1]
    return [
        jnp.transpose(jnp.broadcast_to(taps[j : j + 1, :], (LANES, chans)))
        for j in range(taps.shape[0])
    ]


def short_taps(keys, taps):
    lane = lane_ids(keys.shape)
    once = jnp.where(lane < 1, 0.0, pltpu.roll(keys, 1, 1))
    twice = jnp.where(lane < 2, 0.0, pltpu.roll(keys, 2, 1))
    wide = [jnp.concatenate([t] * (keys.shape[1] // LANES), 1) for t in taps]
    return wide[0] * keys + wide[1] * once + wide[2] * twice


def pack_body(
    own, blocks, order, grad_out, query, keys, values, taps, out, held, few, scratch, edge, rows, sems
):
    copies = [pltpu.make_async_copy(taps, few, sems.at[4])] + [
        pltpu.make_async_copy(source.at[0], held.at[i], sems.at[i])
        for i, source in enumerate((keys, values, grad_out, query))
    ]
    for copy in copies:
        copy.start()
    chunk = 2 * own * blocks + 1
    chans, span = keys.shape[1:]
    peers = chans // own
    copies[0].wait()
    tap = tap_tiles(few)
    copies[1].wait()
    copies[2].wait()
    key, value = held[0], held[1]
    gated = short_taps(key, tap) * value
    lane = lane_ids((chans, LANES))
    tail = key[:, span - LANES :]
    after = tap[2] * pltpu.roll(tail, 2, 1) + jnp.where(
        lane < 1, tap[1] * pltpu.roll(tail, 1, 1), 0.0
    )
    head = jnp.where(lane < 4, pltpu.roll(value[:, :LANES], 2, 1), 0.0)
    edge[...] = sorted_rows(jnp.where(lane < 2, after, head), order, own)
    for j in range(blocks):
        scratch[0, j] = sorted_rows(gated[:, j * LANES : (j + 1) * LANES], order, own)
    copies[3].wait()
    copies[4].wait()
    for j in range(blocks):
        here = slice(j * LANES, (j + 1) * LANES)
        scratch[1, j] = sorted_rows(held[2, :, here] * held[3, :, here], order, own)
    half = peers // 2
    writes = []
    for part in range(2):
        start = part * half * chunk
        lines = lambda c: pl.ds(part * half * own + c, half, stride=own)
        for t in range(2):
            for j in range(blocks):
                for c in range(own):
                    place = start + 2 * own * j + own * t + c
                    rows[pl.ds(place, half, stride=chunk), :] = scratch[t, j, lines(c), :]
        ends = edge[lines(0), :]
        for c in range(1, own):
            ends = ends + pltpu.roll(edge[lines(c), :], 4 * c, 1)
        rows[pl.ds(start + chunk - 1, half, stride=chunk), :] = ends
        piece = pl.ds(start, half * chunk)
        writes.append(pltpu.make_async_copy(rows.at[piece], out.at[piece], sems.at[5 + part]))
        writes[-1].start()
    for write in writes:
        write.wait()


def filter_body(order, long_filter, first, second, mid, spec, scratch, lhs):
    own, length = long_filter.shape
    rows = length // LANES
    for n, place in enumerate(order):
        scratch[pl.ds(own * n, own), :] = long_filter[:, pl.ds(place * LANES, LANES)]
    signals = [scratch[pl.ds(c, rows, stride=own), :] for c in range(own)]
    spec[...] = forward(signals, first, second, mid, lhs, 0)


def main_body(
    own, blocks, order, recv, filt, first, second, second_inv, first_inv, mid, out, cross, past, next_, lhs, back
):
    chunk = 2 * own * blocks + 1
    peers = recv.shape[0] // chunk
    rows = peers * blocks
    place = lambda t, j, c: pl.ds(2 * own * j + own * t + c, peers, stride=chunk)
    ends = recv[pl.ds(chunk - 1, peers, stride=chunk), :]
    lane = lane_ids(ends.shape)
    for i, s in enumerate(order):
        row = jnp.zeros((1, LANES), F32)
        if s:
            row = recv[pl.ds(chunk * order.index(s - 1) + chunk - 1, 1), :]
        past[pl.ds(i, 1), :] = row
    before = past[...]
    heads, gates, grads = [], [], []
    for c in range(own):
        heads.append(
            jnp.where(lane < 2, pltpu.roll(ends, (LANES - 4 * c - 2) % LANES, 1), 0.0)
        )
        mine = pltpu.roll(before, (LANES - 4 * c) % LANES, 1) if c else before
        tiles = [recv[place(0, j, c), :] for j in range(blocks)]
        tiles[0] = tiles[0] + heads[c] * mine
        gates.append(jnp.concatenate(tiles, 0))
        grads.append(jnp.concatenate([recv[place(1, j, c), :] for j in range(blocks)], 0))
    spec = forward(gates + grads, first, second, mid, lhs, 0)
    gate, grad = spec[: own * rows], spec[own * rows :]
    for c in range(own):
        here = slice(c * rows, (c + 1) * rows)
        g_re, g_im = gate[here, :LANES], gate[here, LANES:]
        d_re, d_im = grad[here, :LANES], grad[here, LANES:]
        f_re, f_im = filt[here, :LANES], filt[here, LANES:]
        put_cut(back, c * rows, g_re * f_re - g_im * f_im, g_re * f_im + g_im * f_re)
        put_cut(back, (own + c) * rows, d_re * f_re + d_im * f_im, d_im * f_re - d_re * f_im)
        cross[here, :LANES] = d_re * g_re + d_im * g_im
        cross[here, LANES:] = d_im * g_re - d_re * g_im
    signals = backward(2 * own, rows, second_inv, first_inv, mid, back, 0)
    for q, signal in enumerate(signals):
        for j in range(blocks):
            out[place(q // own, j, q % own), :] = signal[j * peers : (j + 1) * peers]
    behind = signals[own][:peers] * heads[0]
    for c in range(1, own):
        behind = behind + pltpu.roll(signals[own + c][:peers] * heads[c], 4 * c, 1)
    past[...] = behind
    for i, s in enumerate(order):
        row = jnp.zeros((1, LANES), F32)
        if s + 1 < peers:
            row = past[pl.ds(order.index(s + 1), 1), :]
        next_[pl.ds(i, 1), :] = row
    out[pl.ds(chunk - 1, peers, stride=chunk), :] = jnp.where(
        lane % 4 < 2, next_[...], pltpu.roll(before, 2, 1)
    )


def cross_body(order, cross, second_inv, first_inv, mid, part, scratch, lhs):
    own, length = part.shape
    rows = length // LANES
    for c in range(own):
        here = slice(c * rows, (c + 1) * rows)
        put_cut(lhs, c * rows, cross[here, :LANES], cross[here, LANES:])
    for c, signal in enumerate(backward(own, rows, second_inv, first_inv, mid, lhs, 0)):
        scratch[pl.ds(c, rows, stride=own), :] = signal
    for n, place in enumerate(order):
        part[:, pl.ds(place * LANES, LANES)] = scratch[pl.ds(own * n, own), :]


def finish_body(
    own, blocks, order, recv, grad_out, keys, values, taps, grad_query, grad_keys, grad_values, scratch, edge, held, sems
):
    chunk = 2 * own * blocks + 1
    tap = tap_tiles(taps)
    chans, span = keys.shape[1:]
    peers = chans // own
    lane = lane_ids((chans, LANES))
    tile = lambda x, j: x[0, :, j * LANES : (j + 1) * LANES]

    def gathered(t, j):
        for c in range(own):
            scratch[t, j, pl.ds(c, peers, stride=own), :] = recv[
                pl.ds(2 * own * j + own * t + c, peers, stride=chunk), :
            ]
        return sorted_rows(scratch[t, j], order, own, back=True)

    writes = [
        pltpu.make_async_copy(held.at[i], out.at[0], sems.at[i])
        for i, out in enumerate((grad_query, grad_values, grad_keys))
    ]
    for j in range(blocks):
        held[0, :, j * LANES : (j + 1) * LANES] = tile(grad_out, j) * gathered(0, j)
    writes[0].start()
    ends = recv[pl.ds(chunk - 1, peers, stride=chunk), :]
    for c in range(own):
        edge[pl.ds(c, peers, stride=own), :] = (
            pltpu.roll(ends, (LANES - 4 * c) % LANES, 1) if c else ends
        )
    ext = sorted_rows(edge[...], order, own, back=True)
    turned = pltpu.roll(ext, LANES - 2, 1)
    parts = []
    back_one = back_two = None
    for j in range(blocks):
        key = tile(keys, j)
        one, two = pltpu.roll(key, 1, 1), pltpu.roll(key, 2, 1)
        if j:
            once = jnp.where(lane < 1, back_one, one)
            twice = jnp.where(lane < 2, back_two, two)
        else:
            once = jnp.where(lane < 1, 0.0, one)
            twice = jnp.where(lane < 2, 0.0, two)
        back_one, back_two = one, two
        short = tap[0] * key + tap[1] * once + tap[2] * twice
        if not j:
            short = short + jnp.where(lane < 2, turned, 0.0)
        grad = gathered(1, j)
        held[1, :, j * LANES : (j + 1) * LANES] = grad * short
        parts.append(grad * tile(values, j))
    writes[1].start()
    ahead_one, ahead_two = pltpu.roll(ext, LANES - 1, 1), turned
    for j in reversed(range(blocks)):
        one, two = pltpu.roll(parts[j], LANES - 1, 1), pltpu.roll(parts[j], LANES - 2, 1)
        once = jnp.where(lane < LANES - 1, one, ahead_one)
        twice = jnp.where(lane < LANES - 2, two, ahead_two)
        ahead_one, ahead_two = one, two
        held[2, :, j * LANES : (j + 1) * LANES] = (
            tap[0] * parts[j] + tap[1] * once + tap[2] * twice
        )
    writes[2].start()
    for write in writes:
        write.wait()


def call(body, name, outs, scratch, args, flops, room=32, **specs):
    moved = sum(a.size * a.dtype.itemsize for a in args) + sum(
        math.prod(o.shape) * o.dtype.itemsize for o in outs
    )
    return pl.pallas_call(
        body,
        out_shape=outs,
        scratch_shapes=scratch,
        name=name,
        **specs,
        cost_estimate=pl.CostEstimate(flops=flops, bytes_accessed=moved, transcendentals=0),
        compiler_params=pltpu.CompilerParams(vmem_limit_bytes=room * 2**20),
    )(*args)


def shape(*dims):
    return jax.ShapeDtypeStruct(dims, F32)


def exchange(x, order):
    parts = len(order)
    moved = x.reshape(parts, x.shape[0] // parts, 1, LANES)
    moved = lax.all_to_all(moved, "ctx", split_axis=0, concat_axis=0, axis_index_groups=[order], tiled=True)
    return moved.reshape(x.shape)


def shards(grad_out, query, keys, values, long_filter, short_filter):
    _, chans, span = keys.shape
    own, length = long_filter.shape
    parts = length // span
    blocks = span // LANES
    rows = length // LANES
    assert chans == own * parts and rows == LANES and blocks == own
    packed_rows = parts * (2 * own * blocks + 1)
    order = peer_order(parts)
    places = row_order(order, blocks)
    tables = make_tables(rows, LANES, places)
    taps = short_filter.T
    first, second, second_inv, first_inv, mid = (jnp.asarray(t) for t in tables)
    wide = 6 * LANES
    work = 6 * own * rows * wide * 2 * LANES
    in_hbm = pl.BlockSpec(memory_space=pltpu.HBM)
    tiles = pltpu.VMEM((2, blocks, chans, LANES), F32)
    packed = call(
        functools.partial(pack_body, own, blocks, order),
        "pack",
        (shape(packed_rows, LANES),),
        [
            pltpu.VMEM((4, chans, span), F32),
            pltpu.VMEM(taps.shape, F32),
            tiles,
            pltpu.VMEM((chans, LANES), F32),
            pltpu.VMEM((packed_rows, LANES), F32),
            pltpu.SemaphoreType.DMA((7,)),
        ],
        (grad_out, query, keys, values, taps),
        10 * chans * span,
        60,
        in_specs=[in_hbm] * 5,
        out_specs=(in_hbm,),
    )[0]
    received = exchange(packed, order)
    spec = call(
        functools.partial(filter_body, places),
        "filter_spectrum",
        (shape(own * rows, 2 * LANES),),
        [pltpu.VMEM((own * rows, LANES), F32), pltpu.VMEM((own * rows, wide), BF16)],
        (long_filter, first, second, mid),
        work,
    )[0]
    sent, cross = call(
        functools.partial(main_body, own, blocks, order),
        "main",
        (shape(packed_rows, LANES), shape(own * rows, 2 * LANES)),
        [pltpu.VMEM((parts, LANES), F32)] * 2 + [pltpu.VMEM((2 * own * rows, wide), BF16)] * 2,
        (received, spec, first, second, second_inv, first_inv, mid),
        4 * work,
    )
    returned = exchange(sent, order)
    part = call(
        functools.partial(cross_body, places),
        "cross",
        (shape(own, length),),
        [pltpu.VMEM((own * rows, LANES), F32), pltpu.VMEM((own * rows, wide), BF16)],
        (cross, second_inv, first_inv, mid),
        work,
    )[0]
    grad_long = part + lax.ppermute(part, "seq", [(0, 1), (1, 0)])
    grad_query, grad_keys, grad_values = call(
        functools.partial(finish_body, own, blocks, order),
        "finish",
        (shape(*keys.shape),) * 3,
        [
            tiles,
            pltpu.VMEM((chans, LANES), F32),
            pltpu.VMEM((3, chans, span), F32),
            pltpu.SemaphoreType.DMA((3,)),
        ],
        (returned, grad_out, keys, values, taps),
        10 * chans * span,
        out_specs=(in_hbm,) * 3,
    )
    return grad_query, grad_keys, grad_values, grad_long


def solution(mesh):
    block = P("seq", "ch", "ctx")
    rows = P(("ch", "ctx"), None)
    return jax.shard_map(
        shards,
        mesh=mesh,
        in_specs=(block, block, block, block, rows, P("ch", None)),
        out_specs=(block, block, block, rows),
        check_vma=False,
    )
```

```python
import functools
import math

import jax
import jax.numpy as jnp
import numpy as np
from jax import lax
from jax.experimental import pallas as pl
from jax.experimental.pallas import tpu as pltpu
from jax.sharding import PartitionSpec as P

LANES = 128
F32 = jnp.float32
BF16 = jnp.bfloat16


def halves(table):
    high = table.astype(np.float32).astype(jnp.bfloat16)
    low = (table - high.astype(np.float64)).astype(np.float32).astype(jnp.bfloat16)
    return high, low


CORES = 2


def peer_order(parts):
    planes = parts // CORES // 2
    chips = [y * planes + z for z in reversed(range(planes)) for y in range(2)]
    return [CORES * chip + core for chip in chips for core in range(CORES)]


def row_order(order, blocks):
    return [blocks * s + j for j in range(blocks) for s in order]


def sorted_rows(x, order, own, back=False):
    size = CORES * own
    chips = [s // CORES for s in order[::CORES]]
    assert [CORES * chip + core for chip in chips for core in range(CORES)] == list(order)
    if back:
        chips = [chips.index(k) for k in range(len(chips))]
    return jnp.concatenate([x[size * k : size * (k + 1)] for k in chips], 0)


def make_tables(rows, cols, order):
    length = rows * cols
    shifted = np.arange(rows) + 0.25
    turn_one = 2 * np.pi * np.outer(shifted, np.array(order)) / rows
    turn_mid = 2 * np.pi * np.outer(shifted, np.arange(cols)) / length
    turn_two = 2 * np.pi * np.outer(np.arange(cols), np.arange(cols)) / cols
    cos, sin = np.cos(turn_two), np.sin(turn_two)
    first = np.concatenate([np.cos(turn_one), -np.sin(turn_one)], 0)
    second = np.block([[cos, -sin], [sin, cos]])
    second_inv = np.block([[cos, sin], [-sin, cos]])
    scale = length**-1.5
    first_inv = np.concatenate([np.cos(turn_one).T, -np.sin(turn_one).T], 1) * scale
    both = lambda m: np.concatenate(halves(m), 0)
    mid = np.concatenate([np.cos(turn_mid), -np.sin(turn_mid)], 1).astype(np.float32)
    left = lambda m: np.concatenate([halves(m)[0], halves(m)[0], halves(m)[1]], 1)
    return left(first), both(second), both(second_inv), both(first_inv), mid


def cut(x):
    high = x.astype(BF16)
    return high, (x - high.astype(F32)).astype(BF16)


def dot(a, b):
    return jnp.dot(a, b, preferred_element_type=F32)


def lane_ids(shape):
    return lax.broadcasted_iota(jnp.int32, shape, len(shape) - 1)


def row_ids(shape):
    return lax.broadcasted_iota(jnp.int32, shape, 0)


def put_cut(lhs, row, re, im):
    n = re.shape[0]
    re_hi, re_lo = cut(re)
    im_hi, im_lo = cut(im)
    for place, piece in enumerate((re_hi, im_hi, re_lo, im_lo)):
        lhs[pl.ds(row, n), pl.ds(place * LANES, LANES)] = piece


def left_dot(table, x):
    hi, lo = cut(x)
    rows = table.shape[0] // 2
    twice = dot(table[...], hi)
    return twice[:rows] + (twice[rows:] + dot(table[:rows], lo))


def rows_dot(lhs, row, count, table):
    half = count // 2
    wide = 2 * LANES
    parts = []
    for k in range(2):
        x = lhs[pl.ds(row + k * half, half), :]
        high, low = x[:, :wide], x[:, wide:]
        parts.append(
            dot(high, table[:wide]) + dot(low, table[:wide]) + dot(high, table[wide:])
        )
    return jnp.concatenate(parts, 0)


def forward(signals, first, second, mid, lhs, row):
    rows = signals[0].shape[0]
    turn_re = mid[:, :LANES]
    turn_im = mid[:, LANES:]
    for pair in range(0, len(signals), 2):
        hi, lo = cut(jnp.concatenate(signals[pair : pair + 2], 1))
        part = dot(first[:, : 2 * rows], jnp.concatenate([hi, lo], 0)) + dot(
            first[:, 2 * rows :], hi
        )
        for which in range(2):
            re = part[:rows, which * LANES : (which + 1) * LANES]
            im = part[rows:, which * LANES : (which + 1) * LANES]
            put_cut(
                lhs,
                row + (pair + which) * rows,
                re * turn_re - im * turn_im,
                re * turn_im + im * turn_re,
            )
    return rows_dot(lhs, row, len(signals) * rows, second)


def backward(count, rows, second_inv, first_inv, mid, lhs, row):
    turn_re = mid[:, :LANES]
    turn_im = mid[:, LANES:]
    back = rows_dot(lhs, row, count * rows, second_inv)
    signals = []
    for pair in range(0, count, 2):
        columns = []
        for which in range(2):
            here = back[(pair + which) * rows : (pair + which + 1) * rows]
            re, im = here[:, :LANES], here[:, LANES:]
            columns.append(
                jnp.concatenate([re * turn_re + im * turn_im, im * turn_re - re * turn_im], 0)
            )
        out = left_dot(first_inv, jnp.concatenate(columns, 1))
        signals += [out[:, :LANES], out[:, LANES:]]
    return signals


def tap_tiles(taps):
    chans = taps.shape[1]
    return [
        jnp.transpose(jnp.broadcast_to(taps[j : j + 1, :], (LANES, chans)))
        for j in range(taps.shape[0])
    ]


def short_taps(keys, taps):
    lane = lane_ids(keys.shape)
    once = jnp.where(lane < 1, 0.0, pltpu.roll(keys, 1, 1))
    twice = jnp.where(lane < 2, 0.0, pltpu.roll(keys, 2, 1))
    wide = [jnp.concatenate([t] * (keys.shape[1] // LANES), 1) for t in taps]
    return wide[0] * keys + wide[1] * once + wide[2] * twice


def pack_body(
    own, blocks, order, grad_out, query, keys, values, taps, out, held, few, scratch, edge, rows, sems
):
    copies = [pltpu.make_async_copy(taps, few, sems.at[4])] + [
        pltpu.make_async_copy(source.at[0], held.at[i], sems.at[i])
        for i, source in enumerate((keys, values, grad_out, query))
    ]
    for copy in copies:
        copy.start()
    chunk = 2 * own * blocks + 1
    chans, span = keys.shape[1:]
    peers = chans // own
    copies[0].wait()
    tap = tap_tiles(few)
    copies[1].wait()
    copies[2].wait()
    key, value = held[0], held[1]
    gated = short_taps(key, tap) * value
    lane = lane_ids((chans, LANES))
    tail = key[:, span - LANES :]
    after = tap[2] * pltpu.roll(tail, 2, 1) + jnp.where(
        lane < 1, tap[1] * pltpu.roll(tail, 1, 1), 0.0
    )
    head = jnp.where(lane < 4, pltpu.roll(value[:, :LANES], 2, 1), 0.0)
    edge[...] = sorted_rows(jnp.where(lane < 2, after, head), order, own)
    for j in range(blocks):
        scratch[0, j] = sorted_rows(gated[:, j * LANES : (j + 1) * LANES], order, own)
    copies[3].wait()
    copies[4].wait()
    for j in range(blocks):
        here = slice(j * LANES, (j + 1) * LANES)
        scratch[1, j] = sorted_rows(held[2, :, here] * held[3, :, here], order, own)
    half = peers // 2
    writes = []
    for part in range(2):
        start = part * half * chunk
        lines = lambda c: pl.ds(part * half * own + c, half, stride=own)
        for t in range(2):
            for j in range(blocks):
                for c in range(own):
                    place = start + 2 * own * j + own * t + c
                    rows[pl.ds(place, half, stride=chunk), :] = scratch[t, j, lines(c), :]
        ends = edge[lines(0), :]
        for c in range(1, own):
            ends = ends + pltpu.roll(edge[lines(c), :], 4 * c, 1)
        rows[pl.ds(start + chunk - 1, half, stride=chunk), :] = ends
        piece = pl.ds(start, half * chunk)
        writes.append(pltpu.make_async_copy(rows.at[piece], out.at[piece], sems.at[5 + part]))
        writes[-1].start()
    for write in writes:
        write.wait()


def filter_body(order, long_filter, first, second, mid, spec, scratch, lhs):
    own, length = long_filter.shape
    rows = length // LANES
    for n, place in enumerate(order):
        scratch[pl.ds(own * n, own), :] = long_filter[:, pl.ds(place * LANES, LANES)]
    signals = [scratch[pl.ds(c, rows, stride=own), :] for c in range(own)]
    spec[...] = forward(signals, first, second, mid, lhs, 0)


def main_body(
    own, blocks, order, recv, filt, first, second, second_inv, first_inv, mid, out, cross, past, next_, lhs, back
):
    chunk = 2 * own * blocks + 1
    peers = recv.shape[0] // chunk
    rows = peers * blocks
    place = lambda t, j, c: pl.ds(2 * own * j + own * t + c, peers, stride=chunk)
    ends = recv[pl.ds(chunk - 1, peers, stride=chunk), :]
    lane = lane_ids(ends.shape)
    for i, s in enumerate(order):
        row = jnp.zeros((1, LANES), F32)
        if s:
            row = recv[pl.ds(chunk * order.index(s - 1) + chunk - 1, 1), :]
        past[pl.ds(i, 1), :] = row
    before = past[...]
    heads, gates, grads = [], [], []
    for c in range(own):
        heads.append(
            jnp.where(lane < 2, pltpu.roll(ends, (LANES - 4 * c - 2) % LANES, 1), 0.0)
        )
        mine = pltpu.roll(before, (LANES - 4 * c) % LANES, 1) if c else before
        tiles = [recv[place(0, j, c), :] for j in range(blocks)]
        tiles[0] = tiles[0] + heads[c] * mine
        gates.append(jnp.concatenate(tiles, 0))
        grads.append(jnp.concatenate([recv[place(1, j, c), :] for j in range(blocks)], 0))
    spec = forward(gates + grads, first, second, mid, lhs, 0)
    gate, grad = spec[: own * rows], spec[own * rows :]
    for c in range(own):
        here = slice(c * rows, (c + 1) * rows)
        g_re, g_im = gate[here, :LANES], gate[here, LANES:]
        d_re, d_im = grad[here, :LANES], grad[here, LANES:]
        f_re, f_im = filt[here, :LANES], filt[here, LANES:]
        put_cut(back, c * rows, g_re * f_re - g_im * f_im, g_re * f_im + g_im * f_re)
        put_cut(back, (own + c) * rows, d_re * f_re + d_im * f_im, d_im * f_re - d_re * f_im)
        cross[here, :LANES] = d_re * g_re + d_im * g_im
        cross[here, LANES:] = d_im * g_re - d_re * g_im
    signals = backward(2 * own, rows, second_inv, first_inv, mid, back, 0)
    for q, signal in enumerate(signals):
        for j in range(blocks):
            out[place(q // own, j, q % own), :] = signal[j * peers : (j + 1) * peers]
    behind = signals[own][:peers] * heads[0]
    for c in range(1, own):
        behind = behind + pltpu.roll(signals[own + c][:peers] * heads[c], 4 * c, 1)
    past[...] = behind
    for i, s in enumerate(order):
        row = jnp.zeros((1, LANES), F32)
        if s + 1 < peers:
            row = past[pl.ds(order.index(s + 1), 1), :]
        next_[pl.ds(i, 1), :] = row
    out[pl.ds(chunk - 1, peers, stride=chunk), :] = jnp.where(
        lane % 4 < 2, next_[...], pltpu.roll(before, 2, 1)
    )


def cross_body(order, cross, second_inv, first_inv, mid, part, scratch, lhs):
    own, length = part.shape
    rows = length // LANES
    for c in range(own):
        here = slice(c * rows, (c + 1) * rows)
        put_cut(lhs, c * rows, cross[here, :LANES], cross[here, LANES:])
    for c, signal in enumerate(backward(own, rows, second_inv, first_inv, mid, lhs, 0)):
        scratch[pl.ds(c, rows, stride=own), :] = signal
    for n, place in enumerate(order):
        part[:, pl.ds(place * LANES, LANES)] = scratch[pl.ds(own * n, own), :]


def finish_body(
    own, blocks, order, recv, grad_out, keys, values, taps, part, other, grad_query, grad_keys, grad_values, grad_long, scratch, edge, held, total, sems
):
    chunk = 2 * own * blocks + 1
    tap = tap_tiles(taps)
    chans, span = keys.shape[1:]
    peers = chans // own
    lane = lane_ids((chans, LANES))
    tile = lambda x, j: x[0, :, j * LANES : (j + 1) * LANES]

    def gathered(t, j):
        for c in range(own):
            scratch[t, j, pl.ds(c, peers, stride=own), :] = recv[
                pl.ds(2 * own * j + own * t + c, peers, stride=chunk), :
            ]
        return sorted_rows(scratch[t, j], order, own, back=True)

    writes = [
        pltpu.make_async_copy(held.at[i], out.at[0], sems.at[i])
        for i, out in enumerate((grad_query, grad_values, grad_keys))
    ] + [pltpu.make_async_copy(total, grad_long, sems.at[3])]
    total[...] = part[...] + other[...]
    writes[3].start()
    for j in range(blocks):
        held[0, :, j * LANES : (j + 1) * LANES] = tile(grad_out, j) * gathered(0, j)
    writes[0].start()
    ends = recv[pl.ds(chunk - 1, peers, stride=chunk), :]
    for c in range(own):
        edge[pl.ds(c, peers, stride=own), :] = (
            pltpu.roll(ends, (LANES - 4 * c) % LANES, 1) if c else ends
        )
    ext = sorted_rows(edge[...], order, own, back=True)
    turned = pltpu.roll(ext, LANES - 2, 1)
    parts = []
    back_one = back_two = None
    for j in range(blocks):
        key = tile(keys, j)
        one, two = pltpu.roll(key, 1, 1), pltpu.roll(key, 2, 1)
        if j:
            once = jnp.where(lane < 1, back_one, one)
            twice = jnp.where(lane < 2, back_two, two)
        else:
            once = jnp.where(lane < 1, 0.0, one)
            twice = jnp.where(lane < 2, 0.0, two)
        back_one, back_two = one, two
        short = tap[0] * key + tap[1] * once + tap[2] * twice
        if not j:
            short = short + jnp.where(lane < 2, turned, 0.0)
        grad = gathered(1, j)
        held[1, :, j * LANES : (j + 1) * LANES] = grad * short
        parts.append(grad * tile(values, j))
    writes[1].start()
    ahead_one, ahead_two = pltpu.roll(ext, LANES - 1, 1), turned
    for j in reversed(range(blocks)):
        one, two = pltpu.roll(parts[j], LANES - 1, 1), pltpu.roll(parts[j], LANES - 2, 1)
        once = jnp.where(lane < LANES - 1, one, ahead_one)
        twice = jnp.where(lane < LANES - 2, two, ahead_two)
        ahead_one, ahead_two = one, two
        held[2, :, j * LANES : (j + 1) * LANES] = (
            tap[0] * parts[j] + tap[1] * once + tap[2] * twice
        )
    writes[2].start()
    for write in writes:
        write.wait()


def call(body, name, outs, scratch, args, flops, room=32, **specs):
    moved = sum(a.size * a.dtype.itemsize for a in args) + sum(
        math.prod(o.shape) * o.dtype.itemsize for o in outs
    )
    return pl.pallas_call(
        body,
        out_shape=outs,
        scratch_shapes=scratch,
        name=name,
        **specs,
        cost_estimate=pl.CostEstimate(flops=flops, bytes_accessed=moved, transcendentals=0),
        compiler_params=pltpu.CompilerParams(vmem_limit_bytes=room * 2**20),
    )(*args)


def shape(*dims):
    return jax.ShapeDtypeStruct(dims, F32)


def exchange(x, order):
    parts = len(order)
    moved = x.reshape(parts, x.shape[0] // parts, 1, LANES)
    moved = lax.all_to_all(moved, "ctx", split_axis=0, concat_axis=0, axis_index_groups=[order], tiled=True)
    return moved.reshape(x.shape)


def shards(grad_out, query, keys, values, long_filter, short_filter):
    _, chans, span = keys.shape
    own, length = long_filter.shape
    parts = length // span
    blocks = span // LANES
    rows = length // LANES
    assert chans == own * parts and rows == LANES and blocks == own
    packed_rows = parts * (2 * own * blocks + 1)
    order = peer_order(parts)
    places = row_order(order, blocks)
    tables = make_tables(rows, LANES, places)
    taps = short_filter.T
    first, second, second_inv, first_inv, mid = (jnp.asarray(t) for t in tables)
    wide = 4 * LANES
    work = 36 * own * rows * LANES * 2 * LANES
    in_hbm = pl.BlockSpec(memory_space=pltpu.HBM)
    tiles = pltpu.VMEM((2, blocks, chans, LANES), F32)
    packed = call(
        functools.partial(pack_body, own, blocks, order),
        "pack",
        (shape(packed_rows, LANES),),
        [
            pltpu.VMEM((4, chans, span), F32),
            pltpu.VMEM(taps.shape, F32),
            tiles,
            pltpu.VMEM((chans, LANES), F32),
            pltpu.VMEM((packed_rows, LANES), F32),
            pltpu.SemaphoreType.DMA((7,)),
        ],
        (grad_out, query, keys, values, taps),
        10 * chans * span,
        60,
        in_specs=[in_hbm] * 5,
        out_specs=(in_hbm,),
    )[0]
    received = exchange(packed, order)
    spec = call(
        functools.partial(filter_body, places),
        "filter_spectrum",
        (shape(own * rows, 2 * LANES),),
        [pltpu.VMEM((own * rows, LANES), F32), pltpu.VMEM((own * rows, wide), BF16)],
        (long_filter, first, second, mid),
        work,
    )[0]
    sent, cross = call(
        functools.partial(main_body, own, blocks, order),
        "main",
        (shape(packed_rows, LANES), shape(own * rows, 2 * LANES)),
        [pltpu.VMEM((parts, LANES), F32)] * 2 + [pltpu.VMEM((2 * own * rows, wide), BF16)] * 2,
        (received, spec, first, second, second_inv, first_inv, mid),
        4 * work,
    )
    returned = exchange(sent, order)
    part = call(
        functools.partial(cross_body, places),
        "cross",
        (shape(own, length),),
        [pltpu.VMEM((own * rows, LANES), F32), pltpu.VMEM((own * rows, wide), BF16)],
        (cross, second_inv, first_inv, mid),
        work,
    )[0]
    other = lax.ppermute(part, "seq", [(0, 1), (1, 0)])
    grad_query, grad_keys, grad_values, grad_long = call(
        functools.partial(finish_body, own, blocks, order),
        "finish",
        (shape(*keys.shape),) * 3 + (shape(own, length),),
        [
            tiles,
            pltpu.VMEM((chans, LANES), F32),
            pltpu.VMEM((3, chans, span), F32),
            pltpu.VMEM((own, length), F32),
            pltpu.SemaphoreType.DMA((4,)),
        ],
        (returned, grad_out, keys, values, taps, part, other),
        10 * chans * span,
        out_specs=(in_hbm,) * 4,
    )
    return grad_query, grad_keys, grad_values, grad_long


def solution(mesh):
    block = P("seq", "ch", "ctx")
    rows = P(("ch", "ctx"), None)
    return jax.shard_map(
        shards,
        mesh=mesh,
        in_specs=(block, block, block, block, rows, P("ch", None)),
        out_specs=(block, block, block, rows),
        check_vma=False,
    )
```

```python
import functools
import math

import jax
import jax.numpy as jnp
import numpy as np
from jax import lax
from jax.experimental import pallas as pl
from jax.experimental.pallas import tpu as pltpu
from jax.sharding import PartitionSpec as P

LANES = 128
F32 = jnp.float32
BF16 = jnp.bfloat16


def halves(table):
    high = table.astype(np.float32).astype(jnp.bfloat16)
    low = (table - high.astype(np.float64)).astype(np.float32).astype(jnp.bfloat16)
    return high, low


CORES = 2


def peer_order(parts):
    planes = parts // CORES // 2
    half = planes // 2
    chips = [
        y * planes + z + far for z in reversed(range(half)) for far in (half, 0) for y in range(2)
    ]
    return [CORES * chip + core for chip in chips for core in range(CORES)]


def row_order(order, blocks):
    return [blocks * s + j for j in range(blocks) for s in order]


def sorted_rows(x, order, own, back=False):
    size = CORES * own
    chips = [s // CORES for s in order[::CORES]]
    assert [CORES * chip + core for chip in chips for core in range(CORES)] == list(order)
    if back:
        chips = [chips.index(k) for k in range(len(chips))]
    return jnp.concatenate([x[size * k : size * (k + 1)] for k in chips], 0)


def make_tables(rows, cols, order):
    length = rows * cols
    shifted = np.arange(rows) + 0.25
    turn_one = 2 * np.pi * np.outer(shifted, np.array(order)) / rows
    turn_mid = 2 * np.pi * np.outer(shifted, np.arange(cols)) / length
    turn_two = 2 * np.pi * np.outer(np.arange(cols), np.arange(cols)) / cols
    cos, sin = np.cos(turn_two), np.sin(turn_two)
    first = np.concatenate([np.cos(turn_one), -np.sin(turn_one)], 0)
    second = np.block([[cos, -sin], [sin, cos]])
    second_inv = np.block([[cos, sin], [-sin, cos]])
    scale = length**-1.5
    first_inv = np.concatenate([np.cos(turn_one).T, -np.sin(turn_one).T], 1) * scale
    both = lambda m: np.concatenate(halves(m), 0)
    mid = np.concatenate([np.cos(turn_mid), -np.sin(turn_mid)], 1).astype(np.float32)
    left = lambda m: np.concatenate([halves(m)[0], halves(m)[0], halves(m)[1]], 1)
    return left(first), both(second), both(second_inv), both(first_inv), mid


def cut(x):
    high = x.astype(BF16)
    return high, (x - high.astype(F32)).astype(BF16)


def dot(a, b):
    return jnp.dot(a, b, preferred_element_type=F32)


def lane_ids(shape):
    return lax.broadcasted_iota(jnp.int32, shape, len(shape) - 1)


def row_ids(shape):
    return lax.broadcasted_iota(jnp.int32, shape, 0)


def put_cut(lhs, row, re, im):
    n = re.shape[0]
    re_hi, re_lo = cut(re)
    im_hi, im_lo = cut(im)
    for place, piece in enumerate((re_hi, im_hi, re_lo, im_lo)):
        lhs[pl.ds(row, n), pl.ds(place * LANES, LANES)] = piece


def left_dot(table, x):
    hi, lo = cut(x)
    rows = table.shape[0] // 2
    twice = dot(table[...], hi)
    return twice[:rows] + (twice[rows:] + dot(table[:rows], lo))


def rows_dot(lhs, row, count, table):
    half = count // 2
    wide = 2 * LANES
    parts = []
    for k in range(2):
        x = lhs[pl.ds(row + k * half, half), :]
        high, low = x[:, :wide], x[:, wide:]
        parts.append(
            dot(high, table[:wide]) + dot(low, table[:wide]) + dot(high, table[wide:])
        )
    return jnp.concatenate(parts, 0)


def forward(signals, first, second, mid, lhs, row):
    rows = signals[0].shape[0]
    turn_re = mid[:, :LANES]
    turn_im = mid[:, LANES:]
    for pair in range(0, len(signals), 2):
        hi, lo = cut(jnp.concatenate(signals[pair : pair + 2], 1))
        part = dot(first[:, : 2 * rows], jnp.concatenate([hi, lo], 0)) + dot(
            first[:, 2 * rows :], hi
        )
        for which in range(2):
            re = part[:rows, which * LANES : (which + 1) * LANES]
            im = part[rows:, which * LANES : (which + 1) * LANES]
            put_cut(
                lhs,
                row + (pair + which) * rows,
                re * turn_re - im * turn_im,
                re * turn_im + im * turn_re,
            )
    return rows_dot(lhs, row, len(signals) * rows, second)


def backward(count, rows, second_inv, first_inv, mid, lhs, row):
    turn_re = mid[:, :LANES]
    turn_im = mid[:, LANES:]
    back = rows_dot(lhs, row, count * rows, second_inv)
    signals = []
    for pair in range(0, count, 2):
        columns = []
        for which in range(2):
            here = back[(pair + which) * rows : (pair + which + 1) * rows]
            re, im = here[:, :LANES], here[:, LANES:]
            columns.append(
                jnp.concatenate([re * turn_re + im * turn_im, im * turn_re - re * turn_im], 0)
            )
        out = left_dot(first_inv, jnp.concatenate(columns, 1))
        signals += [out[:, :LANES], out[:, LANES:]]
    return signals


def tap_tiles(taps):
    chans = taps.shape[1]
    return [
        jnp.transpose(jnp.broadcast_to(taps[j : j + 1, :], (LANES, chans)))
        for j in range(taps.shape[0])
    ]


def short_taps(keys, taps):
    lane = lane_ids(keys.shape)
    once = jnp.where(lane < 1, 0.0, pltpu.roll(keys, 1, 1))
    twice = jnp.where(lane < 2, 0.0, pltpu.roll(keys, 2, 1))
    wide = [jnp.concatenate([t] * (keys.shape[1] // LANES), 1) for t in taps]
    return wide[0] * keys + wide[1] * once + wide[2] * twice


def pack_body(
    own, blocks, order, grad_out, query, keys, values, taps, out, held, few, scratch, edge, rows, sems
):
    copies = [pltpu.make_async_copy(taps, few, sems.at[4])] + [
        pltpu.make_async_copy(source.at[0], held.at[i], sems.at[i])
        for i, source in enumerate((keys, values, grad_out, query))
    ]
    for copy in copies:
        copy.start()
    chunk = 2 * own * blocks + 1
    chans, span = keys.shape[1:]
    peers = chans // own
    copies[0].wait()
    tap = tap_tiles(few)
    copies[1].wait()
    copies[2].wait()
    key, value = held[0], held[1]
    gated = short_taps(key, tap) * value
    lane = lane_ids((chans, LANES))
    tail = key[:, span - LANES :]
    after = tap[2] * pltpu.roll(tail, 2, 1) + jnp.where(
        lane < 1, tap[1] * pltpu.roll(tail, 1, 1), 0.0
    )
    head = jnp.where(lane < 4, pltpu.roll(value[:, :LANES], 2, 1), 0.0)
    edge[...] = sorted_rows(jnp.where(lane < 2, after, head), order, own)
    for j in range(blocks):
        scratch[0, j] = sorted_rows(gated[:, j * LANES : (j + 1) * LANES], order, own)
    copies[3].wait()
    copies[4].wait()
    for j in range(blocks):
        here = slice(j * LANES, (j + 1) * LANES)
        scratch[1, j] = sorted_rows(held[2, :, here] * held[3, :, here], order, own)
    half = peers // 2
    writes = []
    for part in range(2):
        start = part * half * chunk
        lines = lambda c: pl.ds(part * half * own + c, half, stride=own)
        for t in range(2):
            for j in range(blocks):
                for c in range(own):
                    place = start + 2 * own * j + own * t + c
                    rows[pl.ds(place, half, stride=chunk), :] = scratch[t, j, lines(c), :]
        ends = edge[lines(0), :]
        for c in range(1, own):
            ends = ends + pltpu.roll(edge[lines(c), :], 4 * c, 1)
        rows[pl.ds(start + chunk - 1, half, stride=chunk), :] = ends
        piece = pl.ds(start, half * chunk)
        writes.append(pltpu.make_async_copy(rows.at[piece], out.at[piece], sems.at[5 + part]))
        writes[-1].start()
    for write in writes:
        write.wait()


def filter_body(order, long_filter, first, second, mid, spec, scratch, lhs):
    own, length = long_filter.shape
    rows = length // LANES
    for n, place in enumerate(order):
        scratch[pl.ds(own * n, own), :] = long_filter[:, pl.ds(place * LANES, LANES)]
    signals = [scratch[pl.ds(c, rows, stride=own), :] for c in range(own)]
    spec[...] = forward(signals, first, second, mid, lhs, 0)


def main_body(
    own, blocks, order, recv, filt, first, second, second_inv, first_inv, mid, out, cross, past, next_, lhs, back
):
    chunk = 2 * own * blocks + 1
    peers = recv.shape[0] // chunk
    rows = peers * blocks
    place = lambda t, j, c: pl.ds(2 * own * j + own * t + c, peers, stride=chunk)
    ends = recv[pl.ds(chunk - 1, peers, stride=chunk), :]
    lane = lane_ids(ends.shape)
    for i, s in enumerate(order):
        row = jnp.zeros((1, LANES), F32)
        if s:
            row = recv[pl.ds(chunk * order.index(s - 1) + chunk - 1, 1), :]
        past[pl.ds(i, 1), :] = row
    before = past[...]
    heads, gates, grads = [], [], []
    for c in range(own):
        heads.append(
            jnp.where(lane < 2, pltpu.roll(ends, (LANES - 4 * c - 2) % LANES, 1), 0.0)
        )
        mine = pltpu.roll(before, (LANES - 4 * c) % LANES, 1) if c else before
        tiles = [recv[place(0, j, c), :] for j in range(blocks)]
        tiles[0] = tiles[0] + heads[c] * mine
        gates.append(jnp.concatenate(tiles, 0))
        grads.append(jnp.concatenate([recv[place(1, j, c), :] for j in range(blocks)], 0))
    spec = forward(gates + grads, first, second, mid, lhs, 0)
    gate, grad = spec[: own * rows], spec[own * rows :]
    for c in range(own):
        here = slice(c * rows, (c + 1) * rows)
        g_re, g_im = gate[here, :LANES], gate[here, LANES:]
        d_re, d_im = grad[here, :LANES], grad[here, LANES:]
        f_re, f_im = filt[here, :LANES], filt[here, LANES:]
        put_cut(back, c * rows, g_re * f_re - g_im * f_im, g_re * f_im + g_im * f_re)
        put_cut(back, (own + c) * rows, d_re * f_re + d_im * f_im, d_im * f_re - d_re * f_im)
        cross[here, :LANES] = d_re * g_re + d_im * g_im
        cross[here, LANES:] = d_im * g_re - d_re * g_im
    signals = backward(2 * own, rows, second_inv, first_inv, mid, back, 0)
    for q, signal in enumerate(signals):
        for j in range(blocks):
            out[place(q // own, j, q % own), :] = signal[j * peers : (j + 1) * peers]
    behind = signals[own][:peers] * heads[0]
    for c in range(1, own):
        behind = behind + pltpu.roll(signals[own + c][:peers] * heads[c], 4 * c, 1)
    past[...] = behind
    for i, s in enumerate(order):
        row = jnp.zeros((1, LANES), F32)
        if s + 1 < peers:
            row = past[pl.ds(order.index(s + 1), 1), :]
        next_[pl.ds(i, 1), :] = row
    out[pl.ds(chunk - 1, peers, stride=chunk), :] = jnp.where(
        lane % 4 < 2, next_[...], pltpu.roll(before, 2, 1)
    )


def cross_body(order, cross, second_inv, first_inv, mid, part, scratch, lhs):
    own, length = part.shape
    rows = length // LANES
    for c in range(own):
        here = slice(c * rows, (c + 1) * rows)
        put_cut(lhs, c * rows, cross[here, :LANES], cross[here, LANES:])
    for c, signal in enumerate(backward(own, rows, second_inv, first_inv, mid, lhs, 0)):
        scratch[pl.ds(c, rows, stride=own), :] = signal
    for n, place in enumerate(order):
        part[:, pl.ds(place * LANES, LANES)] = scratch[pl.ds(own * n, own), :]


def finish_body(
    own, blocks, order, recv, grad_out, keys, values, taps, part, other, grad_query, grad_keys, grad_values, grad_long, scratch, edge, held, total, sems
):
    chunk = 2 * own * blocks + 1
    tap = tap_tiles(taps)
    chans, span = keys.shape[1:]
    peers = chans // own
    lane = lane_ids((chans, LANES))
    tile = lambda x, j: x[0, :, j * LANES : (j + 1) * LANES]

    def gathered(t, j):
        for c in range(own):
            scratch[t, j, pl.ds(c, peers, stride=own), :] = recv[
                pl.ds(2 * own * j + own * t + c, peers, stride=chunk), :
            ]
        return sorted_rows(scratch[t, j], order, own, back=True)

    writes = [
        pltpu.make_async_copy(held.at[i], out.at[0], sems.at[i])
        for i, out in enumerate((grad_query, grad_values, grad_keys))
    ] + [pltpu.make_async_copy(total, grad_long, sems.at[3])]
    total[...] = part[...] + other[...]
    writes[3].start()
    for j in range(blocks):
        held[0, :, j * LANES : (j + 1) * LANES] = tile(grad_out, j) * gathered(0, j)
    writes[0].start()
    ends = recv[pl.ds(chunk - 1, peers, stride=chunk), :]
    for c in range(own):
        edge[pl.ds(c, peers, stride=own), :] = (
            pltpu.roll(ends, (LANES - 4 * c) % LANES, 1) if c else ends
        )
    ext = sorted_rows(edge[...], order, own, back=True)
    turned = pltpu.roll(ext, LANES - 2, 1)
    parts = []
    back_one = back_two = None
    for j in range(blocks):
        key = tile(keys, j)
        one, two = pltpu.roll(key, 1, 1), pltpu.roll(key, 2, 1)
        if j:
            once = jnp.where(lane < 1, back_one, one)
            twice = jnp.where(lane < 2, back_two, two)
        else:
            once = jnp.where(lane < 1, 0.0, one)
            twice = jnp.where(lane < 2, 0.0, two)
        back_one, back_two = one, two
        short = tap[0] * key + tap[1] * once + tap[2] * twice
        if not j:
            short = short + jnp.where(lane < 2, turned, 0.0)
        grad = gathered(1, j)
        held[1, :, j * LANES : (j + 1) * LANES] = grad * short
        parts.append(grad * tile(values, j))
    writes[1].start()
    ahead_one, ahead_two = pltpu.roll(ext, LANES - 1, 1), turned
    for j in reversed(range(blocks)):
        one, two = pltpu.roll(parts[j], LANES - 1, 1), pltpu.roll(parts[j], LANES - 2, 1)
        once = jnp.where(lane < LANES - 1, one, ahead_one)
        twice = jnp.where(lane < LANES - 2, two, ahead_two)
        ahead_one, ahead_two = one, two
        held[2, :, j * LANES : (j + 1) * LANES] = (
            tap[0] * parts[j] + tap[1] * once + tap[2] * twice
        )
    writes[2].start()
    for write in writes:
        write.wait()


def call(body, name, outs, scratch, args, flops, room=32, **specs):
    moved = sum(a.size * a.dtype.itemsize for a in args) + sum(
        math.prod(o.shape) * o.dtype.itemsize for o in outs
    )
    return pl.pallas_call(
        body,
        out_shape=outs,
        scratch_shapes=scratch,
        name=name,
        **specs,
        cost_estimate=pl.CostEstimate(flops=flops, bytes_accessed=moved, transcendentals=0),
        compiler_params=pltpu.CompilerParams(vmem_limit_bytes=room * 2**20),
    )(*args)


def shape(*dims):
    return jax.ShapeDtypeStruct(dims, F32)


def exchange(x, order):
    parts = len(order)
    moved = x.reshape(parts, x.shape[0] // parts, 1, LANES)
    moved = lax.all_to_all(moved, "ctx", split_axis=0, concat_axis=0, axis_index_groups=[order], tiled=True)
    return moved.reshape(x.shape)


def shards(grad_out, query, keys, values, long_filter, short_filter):
    _, chans, span = keys.shape
    own, length = long_filter.shape
    parts = length // span
    blocks = span // LANES
    rows = length // LANES
    assert chans == own * parts and rows == LANES and blocks == own
    packed_rows = parts * (2 * own * blocks + 1)
    order = peer_order(parts)
    places = row_order(order, blocks)
    tables = make_tables(rows, LANES, places)
    taps = short_filter.T
    first, second, second_inv, first_inv, mid = (jnp.asarray(t) for t in tables)
    wide = 4 * LANES
    work = 36 * own * rows * LANES * 2 * LANES
    in_hbm = pl.BlockSpec(memory_space=pltpu.HBM)
    tiles = pltpu.VMEM((2, blocks, chans, LANES), F32)
    packed = call(
        functools.partial(pack_body, own, blocks, order),
        "pack",
        (shape(packed_rows, LANES),),
        [
            pltpu.VMEM((4, chans, span), F32),
            pltpu.VMEM(taps.shape, F32),
            tiles,
            pltpu.VMEM((chans, LANES), F32),
            pltpu.VMEM((packed_rows, LANES), F32),
            pltpu.SemaphoreType.DMA((7,)),
        ],
        (grad_out, query, keys, values, taps),
        10 * chans * span,
        60,
        in_specs=[in_hbm] * 5,
        out_specs=(in_hbm,),
    )[0]
    received = exchange(packed, order)
    spec = call(
        functools.partial(filter_body, places),
        "filter_spectrum",
        (shape(own * rows, 2 * LANES),),
        [pltpu.VMEM((own * rows, LANES), F32), pltpu.VMEM((own * rows, wide), BF16)],
        (long_filter, first, second, mid),
        work,
    )[0]
    sent, cross = call(
        functools.partial(main_body, own, blocks, order),
        "main",
        (shape(packed_rows, LANES), shape(own * rows, 2 * LANES)),
        [pltpu.VMEM((parts, LANES), F32)] * 2 + [pltpu.VMEM((2 * own * rows, wide), BF16)] * 2,
        (received, spec, first, second, second_inv, first_inv, mid),
        4 * work,
    )
    returned = exchange(sent, order)
    part = call(
        functools.partial(cross_body, places),
        "cross",
        (shape(own, length),),
        [pltpu.VMEM((own * rows, LANES), F32), pltpu.VMEM((own * rows, wide), BF16)],
        (cross, second_inv, first_inv, mid),
        work,
    )[0]
    other = lax.ppermute(part, "seq", [(0, 1), (1, 0)])
    grad_query, grad_keys, grad_values, grad_long = call(
        functools.partial(finish_body, own, blocks, order),
        "finish",
        (shape(*keys.shape),) * 3 + (shape(own, length),),
        [
            tiles,
            pltpu.VMEM((chans, LANES), F32),
            pltpu.VMEM((3, chans, span), F32),
            pltpu.VMEM((own, length), F32),
            pltpu.SemaphoreType.DMA((4,)),
        ],
        (returned, grad_out, keys, values, taps, part, other),
        10 * chans * span,
        out_specs=(in_hbm,) * 4,
    )
    return grad_query, grad_keys, grad_values, grad_long


def solution(mesh):
    block = P("seq", "ch", "ctx")
    rows = P(("ch", "ctx"), None)
    return jax.shard_map(
        shards,
        mesh=mesh,
        in_specs=(block, block, block, block, rows, P("ch", None)),
        out_specs=(block, block, block, rows),
        check_vma=False,
    )
```

```python
import functools
import math

import jax
import jax.numpy as jnp
import numpy as np
from jax import lax
from jax.experimental import pallas as pl
from jax.experimental.pallas import tpu as pltpu
from jax.sharding import PartitionSpec as P

LANES = 128
F32 = jnp.float32
BF16 = jnp.bfloat16


def halves(table):
    high = table.astype(np.float32).astype(jnp.bfloat16)
    low = (table - high.astype(np.float64)).astype(np.float32).astype(jnp.bfloat16)
    return high, low


CORES = 2


def peer_order(parts):
    planes = parts // CORES // 2
    half = planes // 2
    chips = [
        y * planes + z + far for z in reversed(range(half)) for far in (half, 0) for y in range(2)
    ]
    return [CORES * chip + core for chip in chips for core in range(CORES)]


def row_order(order, blocks):
    return [blocks * s + j for j in range(blocks) for s in order]


def chip_order(order):
    chips = [s // CORES for s in order[::CORES]]
    assert [CORES * chip + core for chip in chips for core in range(CORES)] == list(order)
    return chips


def sorted_rows(x, order, own, back=False):
    size = CORES * own
    chips = chip_order(order)
    if back:
        chips = [chips.index(k) for k in range(len(chips))]
    return jnp.concatenate([x[size * k : size * (k + 1)] for k in chips], 0)


def make_tables(rows, cols, order):
    length = rows * cols
    shifted = np.arange(rows) + 0.25
    turn_one = 2 * np.pi * np.outer(shifted, np.array(order)) / rows
    turn_mid = 2 * np.pi * np.outer(shifted, np.arange(cols)) / length
    turn_two = 2 * np.pi * np.outer(np.arange(cols), np.arange(cols)) / cols
    cos, sin = np.cos(turn_two), np.sin(turn_two)
    first = np.concatenate([np.cos(turn_one), -np.sin(turn_one)], 0)
    second = np.block([[cos, -sin], [sin, cos]])
    second_inv = np.block([[cos, sin], [-sin, cos]])
    scale = length**-1.5
    first_inv = np.concatenate([np.cos(turn_one).T, -np.sin(turn_one).T], 1) * scale
    both = lambda m: np.concatenate(halves(m), 0)
    mid = np.concatenate([np.cos(turn_mid), -np.sin(turn_mid)], 1).astype(np.float32)
    left = lambda m: np.concatenate([halves(m)[0], halves(m)[0], halves(m)[1]], 1)
    return left(first), both(second), both(second_inv), both(first_inv), mid


def cut(x):
    high = x.astype(BF16)
    return high, (x - high.astype(F32)).astype(BF16)


def dot(a, b):
    return jnp.dot(a, b, preferred_element_type=F32)


def lane_ids(shape):
    return lax.broadcasted_iota(jnp.int32, shape, len(shape) - 1)


def row_ids(shape):
    return lax.broadcasted_iota(jnp.int32, shape, 0)


def put_cut(lhs, row, re, im):
    n = re.shape[0]
    re_hi, re_lo = cut(re)
    im_hi, im_lo = cut(im)
    for place, piece in enumerate((re_hi, im_hi, re_lo, im_lo)):
        lhs[pl.ds(row, n), pl.ds(place * LANES, LANES)] = piece


def left_dot(table, x):
    hi, lo = cut(x)
    rows = table.shape[0] // 2
    twice = dot(table[...], hi)
    return twice[:rows] + (twice[rows:] + dot(table[:rows], lo))


def rows_dot(lhs, row, count, table):
    half = count // 2
    wide = 2 * LANES
    parts = []
    for k in range(2):
        x = lhs[pl.ds(row + k * half, half), :]
        high, low = x[:, :wide], x[:, wide:]
        parts.append(
            dot(high, table[:wide]) + dot(low, table[:wide]) + dot(high, table[wide:])
        )
    return jnp.concatenate(parts, 0)


def forward(signals, first, second, mid, lhs, row):
    rows = signals[0].shape[0]
    turn_re = mid[:, :LANES]
    turn_im = mid[:, LANES:]
    for pair in range(0, len(signals), 2):
        hi, lo = cut(jnp.concatenate(signals[pair : pair + 2], 1))
        part = dot(first[:, : 2 * rows], jnp.concatenate([hi, lo], 0)) + dot(
            first[:, 2 * rows :], hi
        )
        for which in range(2):
            re = part[:rows, which * LANES : (which + 1) * LANES]
            im = part[rows:, which * LANES : (which + 1) * LANES]
            put_cut(
                lhs,
                row + (pair + which) * rows,
                re * turn_re - im * turn_im,
                re * turn_im + im * turn_re,
            )
    return rows_dot(lhs, row, len(signals) * rows, second)


def backward(count, rows, second_inv, first_inv, mid, lhs, row):
    turn_re = mid[:, :LANES]
    turn_im = mid[:, LANES:]
    back = rows_dot(lhs, row, count * rows, second_inv)
    signals = []
    for pair in range(0, count, 2):
        columns = []
        for which in range(2):
            here = back[(pair + which) * rows : (pair + which + 1) * rows]
            re, im = here[:, :LANES], here[:, LANES:]
            columns.append(
                jnp.concatenate([re * turn_re + im * turn_im, im * turn_re - re * turn_im], 0)
            )
        out = left_dot(first_inv, jnp.concatenate(columns, 1))
        signals += [out[:, :LANES], out[:, LANES:]]
    return signals


def tap_tiles(taps):
    chans = taps.shape[1]
    return [
        jnp.transpose(jnp.broadcast_to(taps[j : j + 1, :], (LANES, chans)))
        for j in range(taps.shape[0])
    ]


def short_taps(keys, taps):
    lane = lane_ids(keys.shape)
    once = jnp.where(lane < 1, 0.0, pltpu.roll(keys, 1, 1))
    twice = jnp.where(lane < 2, 0.0, pltpu.roll(keys, 2, 1))
    wide = [jnp.concatenate([t] * (keys.shape[1] // LANES), 1) for t in taps]
    return wide[0] * keys + wide[1] * once + wide[2] * twice


def pack_body(
    own, blocks, order, grad_out, query, keys, values, taps, out, held, few, scratch, edge, rows, sems
):
    chunk = 2 * own * blocks + 1
    chans, span = keys.shape[1:]
    peers = chans // own
    size, half = CORES * own, chans // 2
    sources = (keys, values, grad_out, query)
    chips = chip_order(order)
    few_copy = pltpu.make_async_copy(taps, few, sems.at[8])
    few_copy.start()
    for h in range(2):
        for i, source in enumerate(sources):
            for k in range(h * half // size, (h + 1) * half // size):
                pltpu.make_async_copy(
                    source.at[0, pl.ds(size * chips[k], size)],
                    held.at[i, pl.ds(size * k, size)],
                    sems.at[2 * i + h],
                ).start()
    few_copy.wait()
    tap = [sorted_rows(t, order, own) for t in tap_tiles(few)]
    lane = lane_ids((half, LANES))
    writes = []
    for h in range(2):
        mine = pl.ds(h * half, half)
        near = [t[h * half : (h + 1) * half] for t in tap]

        def arrived(i):
            pltpu.make_async_copy(
                sources[i].at[0, pl.ds(0, half)], held.at[i, mine], sems.at[2 * i + h]
            ).wait()

        arrived(0)
        arrived(1)
        key, value = held[0, mine], held[1, mine]
        gated = short_taps(key, near) * value
        tail = key[:, span - LANES :]
        after = near[2] * pltpu.roll(tail, 2, 1) + jnp.where(
            lane < 1, near[1] * pltpu.roll(tail, 1, 1), 0.0
        )
        head = jnp.where(lane < 4, pltpu.roll(value[:, :LANES], 2, 1), 0.0)
        edge[mine, :] = jnp.where(lane < 2, after, head)
        arrived(2)
        arrived(3)
        grad = held[2, mine] * held[3, mine]
        start = h * (peers // 2) * chunk
        lines = lambda c: pl.ds(h * half + c, peers // 2, stride=own)
        for t, whole in enumerate((gated, grad)):
            for j in range(blocks):
                scratch[t, j, mine] = whole[:, j * LANES : (j + 1) * LANES]
                for c in range(own):
                    place = start + 2 * own * j + own * t + c
                    rows[pl.ds(place, peers // 2, stride=chunk), :] = scratch[t, j, lines(c), :]
        ends = edge[lines(0), :]
        for c in range(1, own):
            ends = ends + pltpu.roll(edge[lines(c), :], 4 * c, 1)
        rows[pl.ds(start + chunk - 1, peers // 2, stride=chunk), :] = ends
        piece = pl.ds(start, peers // 2 * chunk)
        writes.append(pltpu.make_async_copy(rows.at[piece], out.at[piece], sems.at[9 + h]))
        writes[-1].start()
    for write in writes:
        write.wait()


def filter_body(order, long_filter, first, second, mid, spec, scratch, lhs):
    own, length = long_filter.shape
    rows = length // LANES
    for n, place in enumerate(order):
        scratch[pl.ds(own * n, own), :] = long_filter[:, pl.ds(place * LANES, LANES)]
    signals = [scratch[pl.ds(c, rows, stride=own), :] for c in range(own)]
    spec[...] = forward(signals, first, second, mid, lhs, 0)


def main_body(
    own, blocks, order, recv, filt, first, second, second_inv, first_inv, mid, out, cross, past, next_, lhs, back
):
    chunk = 2 * own * blocks + 1
    peers = recv.shape[0] // chunk
    rows = peers * blocks
    place = lambda t, j, c: pl.ds(2 * own * j + own * t + c, peers, stride=chunk)
    ends = recv[pl.ds(chunk - 1, peers, stride=chunk), :]
    lane = lane_ids(ends.shape)
    for i, s in enumerate(order):
        row = jnp.zeros((1, LANES), F32)
        if s:
            row = recv[pl.ds(chunk * order.index(s - 1) + chunk - 1, 1), :]
        past[pl.ds(i, 1), :] = row
    before = past[...]
    heads, gates, grads = [], [], []
    for c in range(own):
        heads.append(
            jnp.where(lane < 2, pltpu.roll(ends, (LANES - 4 * c - 2) % LANES, 1), 0.0)
        )
        mine = pltpu.roll(before, (LANES - 4 * c) % LANES, 1) if c else before
        tiles = [recv[place(0, j, c), :] for j in range(blocks)]
        tiles[0] = tiles[0] + heads[c] * mine
        gates.append(jnp.concatenate(tiles, 0))
        grads.append(jnp.concatenate([recv[place(1, j, c), :] for j in range(blocks)], 0))
    spec = forward(gates + grads, first, second, mid, lhs, 0)
    gate, grad = spec[: own * rows], spec[own * rows :]
    for c in range(own):
        here = slice(c * rows, (c + 1) * rows)
        g_re, g_im = gate[here, :LANES], gate[here, LANES:]
        d_re, d_im = grad[here, :LANES], grad[here, LANES:]
        f_re, f_im = filt[here, :LANES], filt[here, LANES:]
        put_cut(back, c * rows, g_re * f_re - g_im * f_im, g_re * f_im + g_im * f_re)
        put_cut(back, (own + c) * rows, d_re * f_re + d_im * f_im, d_im * f_re - d_re * f_im)
        cross[here, :LANES] = d_re * g_re + d_im * g_im
        cross[here, LANES:] = d_im * g_re - d_re * g_im
    signals = backward(2 * own, rows, second_inv, first_inv, mid, back, 0)
    for q, signal in enumerate(signals):
        for j in range(blocks):
            out[place(q // own, j, q % own), :] = signal[j * peers : (j + 1) * peers]
    behind = signals[own][:peers] * heads[0]
    for c in range(1, own):
        behind = behind + pltpu.roll(signals[own + c][:peers] * heads[c], 4 * c, 1)
    past[...] = behind
    for i, s in enumerate(order):
        row = jnp.zeros((1, LANES), F32)
        if s + 1 < peers:
            row = past[pl.ds(order.index(s + 1), 1), :]
        next_[pl.ds(i, 1), :] = row
    out[pl.ds(chunk - 1, peers, stride=chunk), :] = jnp.where(
        lane % 4 < 2, next_[...], pltpu.roll(before, 2, 1)
    )


def cross_body(order, cross, second_inv, first_inv, mid, part, scratch, lhs):
    own, length = part.shape
    rows = length // LANES
    for c in range(own):
        here = slice(c * rows, (c + 1) * rows)
        put_cut(lhs, c * rows, cross[here, :LANES], cross[here, LANES:])
    for c, signal in enumerate(backward(own, rows, second_inv, first_inv, mid, lhs, 0)):
        scratch[pl.ds(c, rows, stride=own), :] = signal
    for n, place in enumerate(order):
        part[:, pl.ds(place * LANES, LANES)] = scratch[pl.ds(own * n, own), :]


def finish_body(
    own, blocks, order, recv, grad_out, keys, values, taps, part, other, grad_query, grad_keys, grad_values, grad_long, scratch, edge, held, total, sems
):
    chunk = 2 * own * blocks + 1
    tap = tap_tiles(taps)
    chans, span = keys.shape[1:]
    peers = chans // own
    lane = lane_ids((chans, LANES))
    tile = lambda x, j: x[0, :, j * LANES : (j + 1) * LANES]

    def gathered(t, j):
        for c in range(own):
            scratch[t, j, pl.ds(c, peers, stride=own), :] = recv[
                pl.ds(2 * own * j + own * t + c, peers, stride=chunk), :
            ]
        return sorted_rows(scratch[t, j], order, own, back=True)

    writes = [
        pltpu.make_async_copy(held.at[i], out.at[0], sems.at[i])
        for i, out in enumerate((grad_query, grad_values, grad_keys))
    ] + [pltpu.make_async_copy(total, grad_long, sems.at[3])]
    total[...] = part[...] + other[...]
    writes[3].start()
    for j in range(blocks):
        held[0, :, j * LANES : (j + 1) * LANES] = tile(grad_out, j) * gathered(0, j)
    writes[0].start()
    ends = recv[pl.ds(chunk - 1, peers, stride=chunk), :]
    for c in range(own):
        edge[pl.ds(c, peers, stride=own), :] = (
            pltpu.roll(ends, (LANES - 4 * c) % LANES, 1) if c else ends
        )
    ext = sorted_rows(edge[...], order, own, back=True)
    turned = pltpu.roll(ext, LANES - 2, 1)
    parts = []
    back_one = back_two = None
    for j in range(blocks):
        key = tile(keys, j)
        one, two = pltpu.roll(key, 1, 1), pltpu.roll(key, 2, 1)
        if j:
            once = jnp.where(lane < 1, back_one, one)
            twice = jnp.where(lane < 2, back_two, two)
        else:
            once = jnp.where(lane < 1, 0.0, one)
            twice = jnp.where(lane < 2, 0.0, two)
        back_one, back_two = one, two
        short = tap[0] * key + tap[1] * once + tap[2] * twice
        if not j:
            short = short + jnp.where(lane < 2, turned, 0.0)
        grad = gathered(1, j)
        held[1, :, j * LANES : (j + 1) * LANES] = grad * short
        parts.append(grad * tile(values, j))
    writes[1].start()
    ahead_one, ahead_two = pltpu.roll(ext, LANES - 1, 1), turned
    for j in reversed(range(blocks)):
        one, two = pltpu.roll(parts[j], LANES - 1, 1), pltpu.roll(parts[j], LANES - 2, 1)
        once = jnp.where(lane < LANES - 1, one, ahead_one)
        twice = jnp.where(lane < LANES - 2, two, ahead_two)
        ahead_one, ahead_two = one, two
        held[2, :, j * LANES : (j + 1) * LANES] = (
            tap[0] * parts[j] + tap[1] * once + tap[2] * twice
        )
    writes[2].start()
    for write in writes:
        write.wait()


def call(body, name, outs, scratch, args, flops, room=32, **specs):
    moved = sum(a.size * a.dtype.itemsize for a in args) + sum(
        math.prod(o.shape) * o.dtype.itemsize for o in outs
    )
    return pl.pallas_call(
        body,
        out_shape=outs,
        scratch_shapes=scratch,
        name=name,
        **specs,
        cost_estimate=pl.CostEstimate(flops=flops, bytes_accessed=moved, transcendentals=0),
        compiler_params=pltpu.CompilerParams(vmem_limit_bytes=room * 2**20),
    )(*args)


def shape(*dims):
    return jax.ShapeDtypeStruct(dims, F32)


def exchange(x, order):
    parts = len(order)
    moved = x.reshape(parts, x.shape[0] // parts, 1, LANES)
    moved = lax.all_to_all(moved, "ctx", split_axis=0, concat_axis=0, axis_index_groups=[order], tiled=True)
    return moved.reshape(x.shape)


def shards(grad_out, query, keys, values, long_filter, short_filter):
    _, chans, span = keys.shape
    own, length = long_filter.shape
    parts = length // span
    blocks = span // LANES
    rows = length // LANES
    assert chans == own * parts and rows == LANES and blocks == own
    packed_rows = parts * (2 * own * blocks + 1)
    order = peer_order(parts)
    places = row_order(order, blocks)
    tables = make_tables(rows, LANES, places)
    taps = short_filter.T
    first, second, second_inv, first_inv, mid = (jnp.asarray(t) for t in tables)
    wide = 4 * LANES
    work = 36 * own * rows * LANES * 2 * LANES
    in_hbm = pl.BlockSpec(memory_space=pltpu.HBM)
    tiles = pltpu.VMEM((2, blocks, chans, LANES), F32)
    packed = call(
        functools.partial(pack_body, own, blocks, order),
        "pack",
        (shape(packed_rows, LANES),),
        [
            pltpu.VMEM((4, chans, span), F32),
            pltpu.VMEM(taps.shape, F32),
            tiles,
            pltpu.VMEM((chans, LANES), F32),
            pltpu.VMEM((packed_rows, LANES), F32),
            pltpu.SemaphoreType.DMA((11,)),
        ],
        (grad_out, query, keys, values, taps),
        10 * chans * span,
        60,
        in_specs=[in_hbm] * 5,
        out_specs=(in_hbm,),
    )[0]
    received = exchange(packed, order)
    spec = call(
        functools.partial(filter_body, places),
        "filter_spectrum",
        (shape(own * rows, 2 * LANES),),
        [pltpu.VMEM((own * rows, LANES), F32), pltpu.VMEM((own * rows, wide), BF16)],
        (long_filter, first, second, mid),
        work,
    )[0]
    sent, cross = call(
        functools.partial(main_body, own, blocks, order),
        "main",
        (shape(packed_rows, LANES), shape(own * rows, 2 * LANES)),
        [pltpu.VMEM((parts, LANES), F32)] * 2 + [pltpu.VMEM((2 * own * rows, wide), BF16)] * 2,
        (received, spec, first, second, second_inv, first_inv, mid),
        4 * work,
    )
    returned = exchange(sent, order)
    part = call(
        functools.partial(cross_body, places),
        "cross",
        (shape(own, length),),
        [pltpu.VMEM((own * rows, LANES), F32), pltpu.VMEM((own * rows, wide), BF16)],
        (cross, second_inv, first_inv, mid),
        work,
    )[0]
    other = lax.ppermute(part, "seq", [(0, 1), (1, 0)])
    grad_query, grad_keys, grad_values, grad_long = call(
        functools.partial(finish_body, own, blocks, order),
        "finish",
        (shape(*keys.shape),) * 3 + (shape(own, length),),
        [
            tiles,
            pltpu.VMEM((chans, LANES), F32),
            pltpu.VMEM((3, chans, span), F32),
            pltpu.VMEM((own, length), F32),
            pltpu.SemaphoreType.DMA((4,)),
        ],
        (returned, grad_out, keys, values, taps, part, other),
        10 * chans * span,
        out_specs=(in_hbm,) * 4,
    )
    return grad_query, grad_keys, grad_values, grad_long


def solution(mesh):
    block = P("seq", "ch", "ctx")
    rows = P(("ch", "ctx"), None)
    return jax.shard_map(
        shards,
        mesh=mesh,
        in_specs=(block, block, block, block, rows, P("ch", None)),
        out_specs=(block, block, block, rows),
        check_vma=False,
    )
```

```python
import functools
import math

import jax
import jax.numpy as jnp
import numpy as np
from jax import lax
from jax.experimental import pallas as pl
from jax.experimental.pallas import tpu as pltpu
from jax.sharding import PartitionSpec as P

LANES = 128
F32 = jnp.float32
BF16 = jnp.bfloat16


def halves(table):
    high = table.astype(np.float32).astype(jnp.bfloat16)
    low = (table - high.astype(np.float64)).astype(np.float32).astype(jnp.bfloat16)
    return high, low


CORES = 2


def peer_order(parts):
    planes = parts // CORES // 2
    half = planes // 2
    chips = [
        y * planes + z + far for z in reversed(range(half)) for far in (half, 0) for y in range(2)
    ]
    return [CORES * chip + core for chip in chips for core in range(CORES)]


def row_order(order, blocks):
    return [blocks * s + j for j in range(blocks) for s in order]


def chip_order(order):
    chips = [s // CORES for s in order[::CORES]]
    assert [CORES * chip + core for chip in chips for core in range(CORES)] == list(order)
    return chips


def sorted_rows(x, order, own, back=False):
    size = CORES * own
    chips = chip_order(order)
    if back:
        chips = [chips.index(k) for k in range(len(chips))]
    return jnp.concatenate([x[size * k : size * (k + 1)] for k in chips], 0)


def make_tables(rows, cols, order):
    length = rows * cols
    shifted = np.arange(rows) + 0.25
    turn_one = 2 * np.pi * np.outer(shifted, np.array(order)) / rows
    turn_mid = 2 * np.pi * np.outer(shifted, np.arange(cols)) / length
    turn_two = 2 * np.pi * np.outer(np.arange(cols), np.arange(cols)) / cols
    cos, sin = np.cos(turn_two), np.sin(turn_two)
    first = np.concatenate([np.cos(turn_one), -np.sin(turn_one)], 0)
    second = np.block([[cos, -sin], [sin, cos]])
    second_inv = np.block([[cos, sin], [-sin, cos]])
    scale = length**-1.5
    first_inv = np.concatenate([np.cos(turn_one).T, -np.sin(turn_one).T], 1) * scale
    both = lambda m: np.concatenate(halves(m), 0)
    mid = np.concatenate([np.cos(turn_mid), -np.sin(turn_mid)], 1).astype(np.float32)
    left = lambda m: np.concatenate([halves(m)[0], halves(m)[0], halves(m)[1]], 1)
    return left(first), both(second), both(second_inv), both(first_inv), mid


def cut(x):
    high = x.astype(BF16)
    return high, (x - high.astype(F32)).astype(BF16)


def dot(a, b):
    return jnp.dot(a, b, preferred_element_type=F32)


def lane_ids(shape):
    return lax.broadcasted_iota(jnp.int32, shape, len(shape) - 1)


def row_ids(shape):
    return lax.broadcasted_iota(jnp.int32, shape, 0)


def put_cut(lhs, row, re, im):
    n = re.shape[0]
    re_hi, re_lo = cut(re)
    im_hi, im_lo = cut(im)
    for place, piece in enumerate((re_hi, im_hi, re_lo, im_lo)):
        lhs[pl.ds(row, n), pl.ds(place * LANES, LANES)] = piece


def left_dot(table, x):
    hi, lo = cut(x)
    rows = table.shape[0] // 2
    twice = dot(table[...], hi)
    return twice[:rows] + (twice[rows:] + dot(table[:rows], lo))


def rows_dot(lhs, row, count, table):
    half = count // 2
    wide = 2 * LANES
    parts = []
    for k in range(2):
        x = lhs[pl.ds(row + k * half, half), :]
        high, low = x[:, :wide], x[:, wide:]
        parts.append(
            dot(high, table[:wide]) + dot(low, table[:wide]) + dot(high, table[wide:])
        )
    return jnp.concatenate(parts, 0)


def forward(signals, first, second, mid, lhs, row):
    rows = signals[0].shape[0]
    turn_re = mid[:, :LANES]
    turn_im = mid[:, LANES:]
    for pair in range(0, len(signals), 2):
        hi, lo = cut(jnp.concatenate(signals[pair : pair + 2], 1))
        part = dot(first[:, : 2 * rows], jnp.concatenate([hi, lo], 0)) + dot(
            first[:, 2 * rows :], hi
        )
        for which in range(2):
            re = part[:rows, which * LANES : (which + 1) * LANES]
            im = part[rows:, which * LANES : (which + 1) * LANES]
            put_cut(
                lhs,
                row + (pair + which) * rows,
                re * turn_re - im * turn_im,
                re * turn_im + im * turn_re,
            )
    return rows_dot(lhs, row, len(signals) * rows, second)


def backward(count, rows, second_inv, first_inv, mid, lhs, row):
    turn_re = mid[:, :LANES]
    turn_im = mid[:, LANES:]
    back = rows_dot(lhs, row, count * rows, second_inv)
    signals = []
    for pair in range(0, count, 2):
        columns = []
        for which in range(2):
            here = back[(pair + which) * rows : (pair + which + 1) * rows]
            re, im = here[:, :LANES], here[:, LANES:]
            columns.append(
                jnp.concatenate([re * turn_re + im * turn_im, im * turn_re - re * turn_im], 0)
            )
        out = left_dot(first_inv, jnp.concatenate(columns, 1))
        signals += [out[:, :LANES], out[:, LANES:]]
    return signals


def tap_tiles(taps):
    chans = taps.shape[1]
    return [
        jnp.transpose(jnp.broadcast_to(taps[j : j + 1, :], (LANES, chans)))
        for j in range(taps.shape[0])
    ]


def short_taps(keys, taps):
    lane = lane_ids(keys.shape)
    once = jnp.where(lane < 1, 0.0, pltpu.roll(keys, 1, 1))
    twice = jnp.where(lane < 2, 0.0, pltpu.roll(keys, 2, 1))
    wide = [jnp.concatenate([t] * (keys.shape[1] // LANES), 1) for t in taps]
    return wide[0] * keys + wide[1] * once + wide[2] * twice


def pack_body(
    own, blocks, order, grad_out, query, keys, values, taps, out, held, few, scratch, edge, rows, sems
):
    chunk = 2 * own * blocks + 1
    chans, span = keys.shape[1:]
    peers = chans // own
    size, half = CORES * own, chans // 2
    sources = (keys, values, grad_out, query)
    chips = chip_order(order)
    few_copy = pltpu.make_async_copy(taps, few, sems.at[8])
    few_copy.start()
    for h in range(2):
        for i, source in enumerate(sources):
            for k in range(h * half // size, (h + 1) * half // size):
                pltpu.make_async_copy(
                    source.at[0, pl.ds(size * chips[k], size)],
                    held.at[i, pl.ds(size * k, size)],
                    sems.at[2 * i + h],
                ).start()
    few_copy.wait()
    tap = [sorted_rows(t, order, own) for t in tap_tiles(few)]
    lane = lane_ids((half, LANES))
    writes = []
    for h in range(2):
        mine = pl.ds(h * half, half)
        near = [t[h * half : (h + 1) * half] for t in tap]

        def arrived(i):
            pltpu.make_async_copy(
                sources[i].at[0, pl.ds(0, half)], held.at[i, mine], sems.at[2 * i + h]
            ).wait()

        arrived(0)
        arrived(1)
        key, value = held[0, mine], held[1, mine]
        gated = short_taps(key, near) * value
        tail = key[:, span - LANES :]
        after = near[2] * pltpu.roll(tail, 2, 1) + jnp.where(
            lane < 1, near[1] * pltpu.roll(tail, 1, 1), 0.0
        )
        head = jnp.where(lane < 4, pltpu.roll(value[:, :LANES], 2, 1), 0.0)
        edge[mine, :] = jnp.where(lane < 2, after, head)
        start = h * (peers // 2) * chunk
        lines = lambda c: pl.ds(h * half + c, peers // 2, stride=own)
        for t in range(2):
            whole = gated
            if t:
                arrived(2)
                arrived(3)
                whole = held[2, mine] * held[3, mine]
            for j in range(blocks):
                scratch[t, j, mine] = whole[:, j * LANES : (j + 1) * LANES]
                for c in range(own):
                    place = start + 2 * own * j + own * t + c
                    rows[pl.ds(place, peers // 2, stride=chunk), :] = scratch[t, j, lines(c), :]
        ends = edge[lines(0), :]
        for c in range(1, own):
            ends = ends + pltpu.roll(edge[lines(c), :], 4 * c, 1)
        rows[pl.ds(start + chunk - 1, peers // 2, stride=chunk), :] = ends
        piece = pl.ds(start, peers // 2 * chunk)
        writes.append(pltpu.make_async_copy(rows.at[piece], out.at[piece], sems.at[9 + h]))
        writes[-1].start()
    for write in writes:
        write.wait()


def filter_body(order, long_filter, first, second, mid, spec, scratch, lhs):
    own, length = long_filter.shape
    rows = length // LANES
    for n, place in enumerate(order):
        scratch[pl.ds(own * n, own), :] = long_filter[:, pl.ds(place * LANES, LANES)]
    signals = [scratch[pl.ds(c, rows, stride=own), :] for c in range(own)]
    spec[...] = forward(signals, first, second, mid, lhs, 0)


def main_body(
    own, blocks, order, recv, filt, first, second, second_inv, first_inv, mid, out, cross, past, next_, lhs, back
):
    chunk = 2 * own * blocks + 1
    peers = recv.shape[0] // chunk
    rows = peers * blocks
    place = lambda t, j, c: pl.ds(2 * own * j + own * t + c, peers, stride=chunk)
    ends = recv[pl.ds(chunk - 1, peers, stride=chunk), :]
    lane = lane_ids(ends.shape)
    for i, s in enumerate(order):
        row = jnp.zeros((1, LANES), F32)
        if s:
            row = recv[pl.ds(chunk * order.index(s - 1) + chunk - 1, 1), :]
        past[pl.ds(i, 1), :] = row
    before = past[...]
    heads, gates, grads = [], [], []
    for c in range(own):
        heads.append(
            jnp.where(lane < 2, pltpu.roll(ends, (LANES - 4 * c - 2) % LANES, 1), 0.0)
        )
        mine = pltpu.roll(before, (LANES - 4 * c) % LANES, 1) if c else before
        tiles = [recv[place(0, j, c), :] for j in range(blocks)]
        tiles[0] = tiles[0] + heads[c] * mine
        gates.append(jnp.concatenate(tiles, 0))
        grads.append(jnp.concatenate([recv[place(1, j, c), :] for j in range(blocks)], 0))
    spec = forward(gates + grads, first, second, mid, lhs, 0)
    gate, grad = spec[: own * rows], spec[own * rows :]
    for c in range(own):
        here = slice(c * rows, (c + 1) * rows)
        g_re, g_im = gate[here, :LANES], gate[here, LANES:]
        d_re, d_im = grad[here, :LANES], grad[here, LANES:]
        f_re, f_im = filt[here, :LANES], filt[here, LANES:]
        put_cut(back, c * rows, g_re * f_re - g_im * f_im, g_re * f_im + g_im * f_re)
        put_cut(back, (own + c) * rows, d_re * f_re + d_im * f_im, d_im * f_re - d_re * f_im)
        cross[here, :LANES] = d_re * g_re + d_im * g_im
        cross[here, LANES:] = d_im * g_re - d_re * g_im
    signals = backward(2 * own, rows, second_inv, first_inv, mid, back, 0)
    for q, signal in enumerate(signals):
        for j in range(blocks):
            out[place(q // own, j, q % own), :] = signal[j * peers : (j + 1) * peers]
    behind = signals[own][:peers] * heads[0]
    for c in range(1, own):
        behind = behind + pltpu.roll(signals[own + c][:peers] * heads[c], 4 * c, 1)
    past[...] = behind
    for i, s in enumerate(order):
        row = jnp.zeros((1, LANES), F32)
        if s + 1 < peers:
            row = past[pl.ds(order.index(s + 1), 1), :]
        next_[pl.ds(i, 1), :] = row
    out[pl.ds(chunk - 1, peers, stride=chunk), :] = jnp.where(
        lane % 4 < 2, next_[...], pltpu.roll(before, 2, 1)
    )


def cross_body(order, cross, second_inv, first_inv, mid, part, scratch, lhs):
    own, length = part.shape
    rows = length // LANES
    for c in range(own):
        here = slice(c * rows, (c + 1) * rows)
        put_cut(lhs, c * rows, cross[here, :LANES], cross[here, LANES:])
    for c, signal in enumerate(backward(own, rows, second_inv, first_inv, mid, lhs, 0)):
        scratch[pl.ds(c, rows, stride=own), :] = signal
    for n, place in enumerate(order):
        part[:, pl.ds(place * LANES, LANES)] = scratch[pl.ds(own * n, own), :]


def finish_body(
    own, blocks, order, recv, grad_out, keys, values, taps, part, other, grad_query, grad_keys, grad_values, grad_long, scratch, edge, held, total, sems
):
    chunk = 2 * own * blocks + 1
    tap = tap_tiles(taps)
    chans, span = keys.shape[1:]
    peers = chans // own
    lane = lane_ids((chans, LANES))
    tile = lambda x, j: x[0, :, j * LANES : (j + 1) * LANES]

    def gathered(t, j):
        for c in range(own):
            scratch[t, j, pl.ds(c, peers, stride=own), :] = recv[
                pl.ds(2 * own * j + own * t + c, peers, stride=chunk), :
            ]
        return sorted_rows(scratch[t, j], order, own, back=True)

    writes = [
        pltpu.make_async_copy(held.at[i], out.at[0], sems.at[i])
        for i, out in enumerate((grad_query, grad_values, grad_keys))
    ] + [pltpu.make_async_copy(total, grad_long, sems.at[3])]
    total[...] = part[...] + other[...]
    writes[3].start()
    for j in range(blocks):
        held[0, :, j * LANES : (j + 1) * LANES] = tile(grad_out, j) * gathered(0, j)
    writes[0].start()
    ends = recv[pl.ds(chunk - 1, peers, stride=chunk), :]
    for c in range(own):
        edge[pl.ds(c, peers, stride=own), :] = (
            pltpu.roll(ends, (LANES - 4 * c) % LANES, 1) if c else ends
        )
    ext = sorted_rows(edge[...], order, own, back=True)
    turned = pltpu.roll(ext, LANES - 2, 1)
    parts = []
    back_one = back_two = None
    for j in range(blocks):
        key = tile(keys, j)
        one, two = pltpu.roll(key, 1, 1), pltpu.roll(key, 2, 1)
        if j:
            once = jnp.where(lane < 1, back_one, one)
            twice = jnp.where(lane < 2, back_two, two)
        else:
            once = jnp.where(lane < 1, 0.0, one)
            twice = jnp.where(lane < 2, 0.0, two)
        back_one, back_two = one, two
        short = tap[0] * key + tap[1] * once + tap[2] * twice
        if not j:
            short = short + jnp.where(lane < 2, turned, 0.0)
        grad = gathered(1, j)
        held[1, :, j * LANES : (j + 1) * LANES] = grad * short
        parts.append(grad * tile(values, j))
    writes[1].start()
    ahead_one, ahead_two = pltpu.roll(ext, LANES - 1, 1), turned
    for j in reversed(range(blocks)):
        one, two = pltpu.roll(parts[j], LANES - 1, 1), pltpu.roll(parts[j], LANES - 2, 1)
        once = jnp.where(lane < LANES - 1, one, ahead_one)
        twice = jnp.where(lane < LANES - 2, two, ahead_two)
        ahead_one, ahead_two = one, two
        held[2, :, j * LANES : (j + 1) * LANES] = (
            tap[0] * parts[j] + tap[1] * once + tap[2] * twice
        )
    writes[2].start()
    for write in writes:
        write.wait()


def call(body, name, outs, scratch, args, flops, room=32, **specs):
    moved = sum(a.size * a.dtype.itemsize for a in args) + sum(
        math.prod(o.shape) * o.dtype.itemsize for o in outs
    )
    return pl.pallas_call(
        body,
        out_shape=outs,
        scratch_shapes=scratch,
        name=name,
        **specs,
        cost_estimate=pl.CostEstimate(flops=flops, bytes_accessed=moved, transcendentals=0),
        compiler_params=pltpu.CompilerParams(vmem_limit_bytes=room * 2**20),
    )(*args)


def shape(*dims):
    return jax.ShapeDtypeStruct(dims, F32)


def exchange(x, order):
    parts = len(order)
    moved = x.reshape(parts, x.shape[0] // parts, 1, LANES)
    moved = lax.all_to_all(moved, "ctx", split_axis=0, concat_axis=0, axis_index_groups=[order], tiled=True)
    return moved.reshape(x.shape)


def shards(grad_out, query, keys, values, long_filter, short_filter):
    _, chans, span = keys.shape
    own, length = long_filter.shape
    parts = length // span
    blocks = span // LANES
    rows = length // LANES
    assert chans == own * parts and rows == LANES and blocks == own
    packed_rows = parts * (2 * own * blocks + 1)
    order = peer_order(parts)
    places = row_order(order, blocks)
    tables = make_tables(rows, LANES, places)
    taps = short_filter.T
    first, second, second_inv, first_inv, mid = (jnp.asarray(t) for t in tables)
    wide = 4 * LANES
    work = 36 * own * rows * LANES * 2 * LANES
    in_hbm = pl.BlockSpec(memory_space=pltpu.HBM)
    tiles = pltpu.VMEM((2, blocks, chans, LANES), F32)
    packed = call(
        functools.partial(pack_body, own, blocks, order),
        "pack",
        (shape(packed_rows, LANES),),
        [
            pltpu.VMEM((4, chans, span), F32),
            pltpu.VMEM(taps.shape, F32),
            tiles,
            pltpu.VMEM((chans, LANES), F32),
            pltpu.VMEM((packed_rows, LANES), F32),
            pltpu.SemaphoreType.DMA((11,)),
        ],
        (grad_out, query, keys, values, taps),
        10 * chans * span,
        60,
        in_specs=[in_hbm] * 5,
        out_specs=(in_hbm,),
    )[0]
    received = exchange(packed, order)
    spec = call(
        functools.partial(filter_body, places),
        "filter_spectrum",
        (shape(own * rows, 2 * LANES),),
        [pltpu.VMEM((own * rows, LANES), F32), pltpu.VMEM((own * rows, wide), BF16)],
        (long_filter, first, second, mid),
        work,
    )[0]
    sent, cross = call(
        functools.partial(main_body, own, blocks, order),
        "main",
        (shape(packed_rows, LANES), shape(own * rows, 2 * LANES)),
        [pltpu.VMEM((parts, LANES), F32)] * 2 + [pltpu.VMEM((2 * own * rows, wide), BF16)] * 2,
        (received, spec, first, second, second_inv, first_inv, mid),
        4 * work,
    )
    returned = exchange(sent, order)
    part = call(
        functools.partial(cross_body, places),
        "cross",
        (shape(own, length),),
        [pltpu.VMEM((own * rows, LANES), F32), pltpu.VMEM((own * rows, wide), BF16)],
        (cross, second_inv, first_inv, mid),
        work,
    )[0]
    other = lax.ppermute(part, "seq", [(0, 1), (1, 0)])
    grad_query, grad_keys, grad_values, grad_long = call(
        functools.partial(finish_body, own, blocks, order),
        "finish",
        (shape(*keys.shape),) * 3 + (shape(own, length),),
        [
            tiles,
            pltpu.VMEM((chans, LANES), F32),
            pltpu.VMEM((3, chans, span), F32),
            pltpu.VMEM((own, length), F32),
            pltpu.SemaphoreType.DMA((4,)),
        ],
        (returned, grad_out, keys, values, taps, part, other),
        10 * chans * span,
        out_specs=(in_hbm,) * 4,
    )
    return grad_query, grad_keys, grad_values, grad_long


def solution(mesh):
    block = P("seq", "ch", "ctx")
    rows = P(("ch", "ctx"), None)
    return jax.shard_map(
        shards,
        mesh=mesh,
        in_specs=(block, block, block, block, rows, P("ch", None)),
        out_specs=(block, block, block, rows),
        check_vma=False,
    )
```
